32 devices in a mesh: parts: 2 (over x), row: 16 (over z, y, core).
Axes of the slice: x: 2, y: 2, z: 4, core: 2. Of those that a mesh axis runs over, the one named last changes fastest.
Arguments:
- coords: int32 [4, 3, 512], P('parts'), parts along dimension 0, may hold values from 0 to 7
- labels: int32 [16, 16, 512], P('parts', 'row'), parts along dimension 0, may hold values from 0 to 255
- ranks: int32 [16, 16, 2], P('parts', 'row'), parts along dimension 0, may hold values from 16 to 128, as said below
- u_first: bfloat16 [16, 16, 512, 128], P('parts', 'row'), parts along dimension 0, may hold values from -6 to 6
- v_first: bfloat16 [16, 16, 512, 128], P('parts', 'row'), parts along dimension 0, may hold values from -0.0046875 to 0.0046875
- u_second: bfloat16 [16, 16, 512, 128], P('parts', 'row'), parts along dimension 0, may hold values from -6 to 6
- v_second: bfloat16 [16, 16, 512, 128], P('parts', 'row'), parts along dimension 0, may hold values from -0.01171875 to 0.01171875
Outputs:
- eliminated: float32 [16, 16, 512, 256], P('parts', 'row'), parts along dimension 0
- diagonal_factors: float32 [4, 512, 512], P('parts'), parts along dimension 0
The draws below stay inside these ranges and needn't reach their ends.
There are 2 independent parts, one for each index of `parts`. The reference program is written for one: setup_inputs(seed, part) draws one part's arguments, and reference() takes and returns one part's arrays. A program takes and returns all parts, laid end to end along the dimension named above; each array names one. Nothing has to cross between parts.
Inputs may be any that keep to these rules, and one draw needn't show every extreme that they name: `ranks`: the block of tile 1 in column 0 has rank 128; some block has rank 128 // 8.
All inputs are finite; a program needn't handle non-finite values.
Results may differ from the reference program's by a relative error of at most 0.0003.
Values may be sent and summed in bfloat16 or wider, within the bound.
No kernel may reach another device: no remote copies, remote signals or barrier semaphores. Data moves between devices by JAX's collectives and lax.ppermute only.
A program may use at most 128 MiB of HBM per device.

```python
import math
import jax
import jax.numpy as jnp
from jax import lax

B = 512
RMAX = 128
NRHS = 256
CYCLES = 8
TILES = 128
N_ROW = 16


def draw_ranks(key, part):
    lowest = RMAX // 8
    number = 2 * TILES
    values = jax.random.randint(jax.random.fold_in(key, 11), (number,), lowest, RMAX + 1)
    second_spot = (3 + jax.random.randint(jax.random.fold_in(key, 13), (), 0, number - 1)) % number
    values = values.at[2].set(RMAX).at[second_spot].set(lowest)
    return values.reshape(CYCLES, TILES // CYCLES, 2).astype(jnp.int32)


def factor_entries(key, salt):
    shape = (CYCLES, TILES // CYCLES, B, RMAX)
    values = jnp.clip(jax.random.normal(jax.random.fold_in(key, salt), shape, jnp.float32), -6.0, 6.0)
    return values


def draw_u_first(key, part):
    return factor_entries(key, 21).astype(jnp.bfloat16)


def draw_v_first(key, part):
    return (factor_entries(key, 22) * (0.4 / B)).astype(jnp.bfloat16)


def set_ends(drawn, key, least, largest):
    spot = [jax.random.randint(jax.random.fold_in(key, axis), (), 0, length) for axis, length in enumerate(drawn.shape)]
    longest = drawn.shape.index(max(drawn.shape))
    neighbour = spot[:longest] + [(spot[longest] + 1) % drawn.shape[longest]] + spot[longest + 1:]
    return drawn.at[tuple(spot)].set(least).at[tuple(neighbour)].set(largest)


def level_of(own_key, shape, cuts, least, largest):
    factor_of, own = 1.0, jax.random.fold_in(own_key, 6)
    for axis_at, shards_of in cuts:
        steps = jnp.exp(jax.random.uniform(jax.random.fold_in(own, axis_at), (shards_of,), jnp.float32, least / len(cuts), largest / len(cuts)))
        factor_of = factor_of * jnp.repeat(steps, shape[axis_at] // shards_of).reshape([-1 if axis == axis_at else 1 for axis in range(len(shape))])
    return factor_of


def bell_draw(rng, extent, width, bound, cuts=(), kind=jnp.bfloat16):
    factor_of = level_of(rng, extent, cuts, -0.22, 0.18) if cuts else 1.0
    result = jax.random.normal(rng, extent, jnp.float32) * width * factor_of
    return jnp.minimum(jnp.maximum(result, -bound), bound).astype(kind)


def setup_inputs(seed: int = 0, part: int = 0) -> dict:
    key_of = jax.random.split(jax.random.key(seed), 8)
    part_keys = jax.random.split(jax.random.fold_in(key_of[7], part), 8)
    coords = set_ends(jax.random.randint(part_keys[0], (2, 3, B), 0, 8), jax.random.fold_in(part_keys[0], 1), 0, 7).astype(jnp.int32)
    labels = set_ends(jax.random.randint(part_keys[1], (CYCLES, N_ROW, B), 0, NRHS), jax.random.fold_in(part_keys[1], 1), 0, NRHS - 1).astype(jnp.int32)
    ranks = draw_ranks(jax.random.fold_in(jax.random.fold_in(key_of[7], part), 71), part)
    u_first = draw_u_first(jax.random.fold_in(jax.random.fold_in(key_of[7], part), 71), part)
    v_first = draw_v_first(jax.random.fold_in(jax.random.fold_in(key_of[7], part), 71), part)
    u_second = bell_draw(part_keys[5], (CYCLES, N_ROW, B, RMAX), 1.0, 6.0, ((1, 16),))
    v_second = bell_draw(part_keys[6], (CYCLES, N_ROW, B, RMAX), (0.4 / B), 0.01171875, ((1, 16),))
    return dict(coords=coords, labels=labels, ranks=ranks, u_first=u_first, v_first=v_first, u_second=u_second, v_second=v_second)


highest = lax.Precision.HIGHEST
four_pi = 4.0 * math.pi

def matmul(left, right):
    return jnp.dot(left.astype(jnp.float32), right.astype(jnp.float32), precision=highest, preferred_element_type=jnp.float32)

def kernel_tile(points):
    spots = points.astype(jnp.float32)
    distance = jnp.zeros((spots.shape[1], spots.shape[1]), jnp.float32)
    for dimension in range(3):
        offset = spots[dimension][:, None] - spots[dimension][None, :]
        distance = distance + offset * offset
    return 1.0 / (four_pi * jnp.sqrt(distance + 1.0)) + jnp.eye(spots.shape[1], dtype=jnp.float32)

def onehot(label_row):
    return (label_row[..., None] == jnp.arange(NRHS, dtype=jnp.int32)).astype(jnp.float32)

def triangular(lower, target):
    return lax.linalg.triangular_solve(lower, target, left_side=True, lower=True)

def solve_stack(lower, stack):
    number, height, breadth = stack.shape
    flat = jnp.transpose(stack, (1, 0, 2)).reshape(height, number * breadth)
    solved = triangular(lower, flat)
    return jnp.transpose(solved.reshape(height, number, breadth), (1, 0, 2))

def rank_mask(rank_values, breadth):
    columns = jnp.arange(breadth, dtype=jnp.int32)
    return (columns[None, :] < rank_values[:, None]).astype(jnp.float32)

def second_panel(points, label_row, u_one, w_one, first_sol):
    inner_gram = matmul(w_one.T, w_one)
    diagonal_tile = kernel_tile(points) - matmul(matmul(u_one, inner_gram), u_one.T)
    lower = jnp.linalg.cholesky(diagonal_tile)
    target = onehot(label_row) - matmul(u_one, matmul(w_one.T, first_sol))
    return (lower, triangular(lower, target))

def update(w_tiles, first_sol, second_lower, second_sol, u_one, w_one, label_rows, rank_rows, u0, u1, v1):
    breadth = u0.shape[-1]
    u_zero = u0.astype(jnp.float32)
    u_next = u1.astype(jnp.float32)
    v_next = v1.astype(jnp.float32) * rank_mask(rank_rows[:, 1], breadth)[:, None, :]
    first_weights = jnp.einsum('nbr,bc->nrc', w_tiles, first_sol, precision=highest)
    first_update = jnp.einsum('nbr,nrc->nbc', u_zero, first_weights, precision=highest)
    cross = jnp.einsum('br,nbs->nrs', w_one, w_tiles, precision=highest)
    mixed = -jnp.einsum('br,nrs->nbs', u_one, cross, precision=highest)
    factor = solve_stack(second_lower, jnp.concatenate([v_next, mixed], axis=-1))
    second_weights = jnp.einsum('nbk,bc->nkc', factor, second_sol, precision=highest)
    left_pair = jnp.concatenate([u_next, u_zero], axis=-1)
    second_update = jnp.einsum('nbk,nkc->nbc', left_pair, second_weights, precision=highest)
    return onehot(label_rows) - first_update - second_update

def reference(coords, labels, ranks, u_first, v_first, u_second, v_second):
    first_lower = jnp.linalg.cholesky(kernel_tile(coords[0]))
    first_sol = triangular(first_lower, onehot(labels[0, 0]))
    mask_one = rank_mask(ranks[0, 1, 0:1], RMAX)
    w_one = triangular(first_lower, v_first[0, 1].astype(jnp.float32) * mask_one)
    u_one = u_first[0, 1].astype(jnp.float32)
    second_lower, second_sol = second_panel(coords[1], labels[0, 1], u_one, w_one, first_sol)

    def per_cycle(pieces):
        label_rows, rank_rows, u0, v0, u1, v1 = pieces
        v_zero = v0.astype(jnp.float32) * rank_mask(rank_rows[:, 0], RMAX)[:, None, :]
        w_tiles = solve_stack(first_lower, v_zero)
        return update(w_tiles, first_sol, second_lower, second_sol, u_one, w_one, label_rows, rank_rows, u0, u1, v1)
    updated = lax.map(per_cycle, (labels, ranks, u_first, v_first, u_second, v_second))
    updated = updated.at[0, 0].set(first_sol).at[0, 1].set(second_sol)
    return (updated, jnp.stack([first_lower, second_lower]))
```

```python
import functools
import math

import jax
import jax.numpy as jnp
from jax import lax
from jax.experimental import pallas as pl
from jax.experimental.pallas import tpu as pltpu
from jax.sharding import PartitionSpec as P

NRHS = 256
LANES = 128
SUB = 8
f32 = jnp.float32
bf16 = jnp.bfloat16
highest = lax.Precision.HIGHEST
VMEM = pltpu.VMEM


def nn(left, right):
    return jnp.dot(left, right, precision=highest, preferred_element_type=f32)


def tn(left, right):
    return lax.dot_general(
        left, right, (((0,), (0,)), ((), ())), precision=highest, preferred_element_type=f32
    )


def nt(left, right):
    return lax.dot_general(
        left, right, (((1,), (1,)), ((), ())), precision=highest, preferred_element_type=f32
    )


def parts_of(value, number):
    pieces = []
    for _ in range(number):
        piece = value.astype(bf16)
        pieces.append(piece)
        value = value - piece.astype(f32)
    return pieces


def exact_dot(left, right, dims):
    return lax.dot_general(left, right, (dims, ((), ())), preferred_element_type=f32)


def row_of(value, index):
    return jnp.broadcast_to(value[index : index + 1, :], value.shape)


def column_of(value, index):
    return jnp.broadcast_to(value[:, index : index + 1], value.shape)


def factor_block(rows, put):
    number = len(rows)
    lane = lax.broadcasted_iota(jnp.int32, (SUB, LANES), 1)
    sub = lax.broadcasted_iota(jnp.int32, (SUB, LANES), 0)
    for step in range(number):
        low = SUB * step
        here = (lane >= low) & (lane < low + SUB)
        columns = [[column_of(rows[i], low + c) for c in range(SUB)] for i in range(step, number)]
        pivot = list(columns[0])
        plain = rows[step]
        work = jnp.where(here, jnp.where(lane - low == sub, 1.0, 0.0).astype(f32), plain)
        upper = jnp.zeros((SUB, LANES), f32)
        inverse = jnp.zeros((SUB, LANES), f32)
        for first in range(0, SUB, 2):
            second = first + 1
            left, right = pivot[first], pivot[second]
            a, b, c = row_of(left, first), row_of(left, second), row_of(right, second)
            scale = 1.0 / (a * c - b * b)
            is_first, is_second = sub == first, sub == second
            both = is_first | is_second
            m_first = jnp.where(is_first, -c, jnp.where(is_second, b, left * c - right * b)) * scale
            m_second = jnp.where(is_first, b, jnp.where(is_second, -a, right * a - left * b)) * scale

            def eliminate(value, top, bottom):
                return jnp.where(both, 0.0, value) - m_first * top - m_second * bottom

            w_top, w_bottom = row_of(work, first), row_of(work, second)
            p_top, p_bottom = row_of(plain, first), row_of(plain, second)
            root = lax.rsqrt(a)
            below = b * root
            last = lax.rsqrt(c - below * below)
            upper = jnp.where(
                is_first,
                p_top * root,
                jnp.where(is_second, (p_bottom - below * (p_top * root)) * last, upper),
            )
            inverse = jnp.where(
                is_first,
                w_top * root,
                jnp.where(is_second, (w_bottom - below * (w_top * root)) * last, inverse),
            )
            for other in range(second + 1, SUB):
                pivot[other] = eliminate(
                    pivot[other], row_of(pivot[other], first), row_of(pivot[other], second)
                )
            work = eliminate(work, w_top, w_bottom)
            if second < SUB - 1:
                plain = eliminate(plain, p_top, p_bottom)
        put(step, jnp.where(lane - low >= sub, upper, 0.0), jnp.where(lane - low <= sub, inverse, 0.0))
        solved = [row_of(work, c) for c in range(SUB)]
        for i in range(step + 1, number):
            terms = [columns[i - step][c] * solved[c] for c in range(SUB)]
            while len(terms) > 1:
                terms = [terms[k] + terms[k + 1] for k in range(0, len(terms), 2)]
            rows[i] = jnp.where(here, 0.0, rows[i]) - terms[0]


def factor_tile(matrix, upper, inverse):
    size = matrix.shape[0]
    blocks = size // LANES
    for k in range(blocks):
        low, high = LANES * k, LANES * (k + 1)

        def put(step, upper_rows, inverse_rows):
            at = pl.ds(low + SUB * step, SUB)
            upper[at, low:high] = upper_rows
            inverse[at, low:high] = inverse_rows

        factor_block(
            [matrix[low + SUB * i : low + SUB * (i + 1), low:high] for i in range(LANES // SUB)], put
        )
        corner = inverse[low:high, low:high]
        if k > 0:
            inverse[low:high, :low] = nn(corner, matrix[low:high, :low])
            upper[low:high, :low] = jnp.zeros((LANES, low), f32)
        if k < blocks - 1:
            panel = nn(corner, matrix[low:high, high:])
            upper[low:high, high:] = panel
            inverse[low:high, high:] = jnp.zeros((LANES, size - high), f32)
            matrix[high:, high:] = matrix[high:, high:] - tn(panel, panel)
            if k > 0:
                matrix[high:, :low] = matrix[high:, :low] - tn(panel, inverse[low:high, :low])
            matrix[high:, low:high] = -tn(panel, corner)


def kernel_tile(points):
    size = points.shape[1]
    spots = points.astype(f32)
    square = jnp.sum(spots * spots, axis=0, keepdims=True)
    one = jnp.ones_like(square)
    zero = jnp.zeros((11, size), f32)
    left = jnp.concatenate([spots, square, one, zero], axis=0).astype(bf16)
    right = jnp.concatenate([-2.0 * spots, one, square, zero], axis=0).astype(bf16)
    distance = exact_dot(left, right, ((0,), (0,)))
    row = lax.broadcasted_iota(jnp.int32, (size, size), 0)
    column = lax.broadcasted_iota(jnp.int32, (size, size), 1)
    return lax.rsqrt(distance + 1.0) * (1.0 / (4.0 * math.pi)) + jnp.where(row == column, 1.0, 0.0)


def onehot_rows(label_row):
    size = label_row.shape[1]
    row = lax.broadcasted_iota(jnp.int32, (NRHS, size), 0).astype(f32)
    return jnp.where(row == label_row, 1.0, 0.0).astype(f32)


def store_lower(upper, lower):
    size = upper.shape[0]
    for i in range(0, size, LANES):
        for j in range(0, size, LANES):
            if i >= j:
                lower[i : i + LANES, j : j + LANES] = upper[j : j + LANES, i : i + LANES].T
            else:
                lower[i : i + LANES, j : j + LANES] = jnp.zeros((LANES, LANES), f32)


def first_kernel(coords, diagonal, inverse, matrix, upper, lower, sem):
    matrix[...] = kernel_tile(coords[0])
    factor_tile(matrix, upper, inverse)
    store_lower(upper, lower)
    copy = pltpu.make_async_copy(lower, diagonal.at[0], sem)
    copy.start()
    copy.wait()


def second_kernel(
    coords, shared, inverse, _, diagonal, y_first, y_second, z_first, z_second,
    matrix, upper, lower, last, sem,
):
    size = inverse.shape[0]
    u_one = shared[0:size, :]
    v_one = shared[size : 2 * size, :]
    labels = shared[2 * size : 2 * size + 16, :].astype(f32)
    spread = size // LANES

    def label_row(which):
        return jnp.concatenate(
            [labels[which * spread + i : which * spread + i + 1, :] for i in range(spread)], axis=1
        )

    def two_sided(value_parts, other, dims):
        return sum(exact_dot(piece, other, dims) for piece in reversed(value_parts))

    inverse_parts = parts_of(inverse[...], 3)
    first_b = onehot_rows(label_row(0)).astype(bf16)
    y0 = two_sided(inverse_parts, first_b, ((1,), (1,)))
    y_first[...] = y0
    w_one = two_sided(inverse_parts, v_one, ((1,), (0,)))
    gram = tn(w_one, w_one)
    wide_u = u_one.astype(f32)
    left = nn(wide_u, gram)
    matrix[...] = kernel_tile(coords[1]) - nt(left, wide_u)
    target = onehot_rows(label_row(1)).T - nn(wide_u, tn(w_one, y0))
    z0 = tn(inverse[...], y0)
    p_one = tn(inverse[...], w_one)
    factor_tile(matrix, upper, last)
    store_lower(upper, lower)
    copy = pltpu.make_async_copy(lower, diagonal.at[1], sem)
    copy.start()
    y1 = nn(last[...], target)
    y_second[...] = y1
    z1 = tn(last[...], y1)
    zc = z0 - nn(p_one, tn(wide_u, z1))
    for which, ref in ((zc, z_first), (z1, z_second)):
        big, small = parts_of(which, 2)
        ref[:, :NRHS] = big
        ref[:, NRHS:] = small
    copy.wait()


def tile_kernel(
    position, ranks, labels, u0, v0, u1, v1, y_first, y_second, z_first, z_second, out
):
    step = pl.program_id(0)

    def weights(v, z, rank):
        both = exact_dot(v[...], z[...], ((0,), (0,)))
        value = both[:, :NRHS] + both[:, NRHS:]
        row = lax.broadcasted_iota(jnp.int32, value.shape, 0)
        return jnp.where(row < rank, value, 0.0)

    h = jnp.concatenate(
        [weights(v0, z_first, ranks[step, 0]), weights(v1, z_second, ranks[step, 1])], axis=0
    )
    big, small = parts_of(h, 2)
    u = jnp.concatenate([u0[...], u1[...]], axis=1)
    total = exact_dot(u, big, ((1,), (0,))) + exact_dot(u, small, ((1,), (0,)))
    size = labels.shape[1]
    column = jnp.broadcast_to(labels[...], (LANES, size)).astype(f32).T
    lane = lax.broadcasted_iota(jnp.int32, (size, LANES), 1).astype(f32)
    hot = jnp.concatenate(
        [jnp.where(column == lane + float(LANES * i), 1.0, 0.0) for i in range(NRHS // LANES)], axis=1
    )
    out[...] = hot - total

    @pl.when((step == 0) & (position[0] == 0))
    def _():
        out[...] = y_first[...]

    @pl.when((step == 0) & (position[0] == 1))
    def _():
        out[...] = y_second[...]


def local(coords, labels, ranks, u_first, v_first, u_second, v_second):
    position = lax.axis_index("row")
    cycles, _, size, breadth = u_first.shape
    whole = pl.BlockSpec(memory_space=VMEM)
    anywhere = pl.BlockSpec(memory_space=pl.ANY)
    params = pltpu.CompilerParams(vmem_limit_bytes=56 << 20)

    kept = jnp.arange(breadth, dtype=jnp.int32)[None, :] < ranks[0, 0, 0]
    v_one = jnp.where(kept & (position == 1), v_first[0, 0], 0)
    u_one = jnp.where(position == 1, u_first[0, 0], 0)
    hot = labels[0, 0].astype(bf16).reshape(size // breadth, breadth)
    payload = jnp.concatenate(
        [
            u_one,
            v_one,
            jnp.where(position == 0, hot, 0),
            jnp.where(position == 1, hot, 0),
            jnp.zeros((8, breadth), bf16),
        ],
        axis=0,
    )
    shared = lax.psum(payload, "row")

    square = jax.ShapeDtypeStruct((size, size), f32)
    tall = jax.ShapeDtypeStruct((size, NRHS), f32)
    pair = jax.ShapeDtypeStruct((size, 2 * NRHS), bf16)
    stack = jax.ShapeDtypeStruct((2, size, size), f32)
    room = [pltpu.VMEM((size, size), f32)] * 3
    diagonal, inverse = pl.pallas_call(
        first_kernel,
        out_shape=[stack, square],
        in_specs=[whole],
        out_specs=[anywhere, whole],
        scratch_shapes=room + [pltpu.SemaphoreType.DMA],
        compiler_params=params,
        cost_estimate=pl.CostEstimate(flops=10**9, bytes_accessed=10**8, transcendentals=0),
        name="first",
    )(coords)
    diagonal, y_first, y_second, z_first, z_second = pl.pallas_call(
        second_kernel,
        out_shape=[stack, tall, tall, pair, pair],
        in_specs=[whole, whole, whole, anywhere],
        out_specs=[anywhere, whole, whole, whole, whole],
        scratch_shapes=room + [pltpu.VMEM((size, size), f32), pltpu.SemaphoreType.DMA],
        input_output_aliases={3: 0},
        compiler_params=params,
        name="second",
    )(coords, shared, inverse, diagonal)

    def tile(width):
        return pl.BlockSpec((None, None, size, width), lambda i, *_: (i, 0, 0, 0))

    def fixed(width):
        return pl.BlockSpec((size, width), lambda i, *_: (0, 0))

    eliminated = pl.pallas_call(
        tile_kernel,
        out_shape=jax.ShapeDtypeStruct((cycles, 1, size, NRHS), f32),
        grid_spec=pltpu.PrefetchScalarGridSpec(
            num_scalar_prefetch=2,
            grid=(cycles,),
            in_specs=[pl.BlockSpec((None, 1, size), lambda i, *_: (i, 0, 0))]
            + [tile(breadth)] * 4
            + [fixed(NRHS)] * 2
            + [fixed(2 * NRHS)] * 2,
            out_specs=tile(NRHS),
        ),
        compiler_params=params,
        name="tiles",
    )(
        position.astype(jnp.int32).reshape(1), ranks[:, 0], labels,
        u_first, v_first, u_second, v_second, y_first, y_second, z_first, z_second,
    )
    return (eliminated, diagonal)


def solution(mesh):
    in_specs = (
        P("parts", None, None),
        P("parts", "row", None),
        P("parts", "row", None),
        P("parts", "row", None, None),
        P("parts", "row", None, None),
        P("parts", "row", None, None),
        P("parts", "row", None, None),
    )
    out_specs = (P("parts", "row", None, None), P("parts", None, None))
    return jax.shard_map(local, mesh=mesh, in_specs=in_specs, out_specs=out_specs, check_vma=False)
```

```python
import functools
import math

import jax
import jax.numpy as jnp
from jax import lax
from jax.experimental import pallas as pl
from jax.experimental.pallas import tpu as pltpu
from jax.sharding import PartitionSpec as P

NRHS = 256
LANES = 128
SUB = 8
HALF = 64
f32 = jnp.float32
bf16 = jnp.bfloat16
highest = lax.Precision.HIGHEST
high = lax.Precision.HIGH
VMEM = pltpu.VMEM
NN, TN, NT = ((1,), (0,)), ((0,), (0,)), ((1,), (1,))


def mul(left, right, dims=NN, precision=None):
    return lax.dot_general(
        left, right, (dims, ((), ())), precision=precision, preferred_element_type=f32
    )


def parts_of(value, number):
    pieces = []
    for _ in range(number):
        piece = value.astype(bf16)
        pieces.append(piece)
        value = value - piece.astype(f32)
    return pieces


def split_left(left, right, dims=NN, number=3):
    return sum(mul(piece, right, dims) for piece in reversed(parts_of(left, number)))


def split_right(left, right, dims=NN, number=3):
    return sum(mul(left, piece, dims) for piece in reversed(parts_of(right, number)))


def row_of(value, index):
    return jnp.broadcast_to(value[index : index + 1, :], value.shape)


def column_of(value, index):
    return jnp.broadcast_to(value[:, index : index + 1], value.shape)


def factor_half(rows, base, put):
    number = len(rows)
    lane = lax.broadcasted_iota(jnp.int32, (SUB, LANES), 1)
    sub = lax.broadcasted_iota(jnp.int32, (SUB, LANES), 0)
    pair = range(2)
    for step in range(0, number, 2):
        low = SUB * (base + step)
        here = (lane >= low) & (lane < low + 2 * SUB)
        columns = [[column_of(rows[i], low + c) for c in range(2 * SUB)] for i in range(step, number)]
        pivot = [list(columns[0]), list(columns[1])]
        plain = [rows[step], rows[step + 1]]
        work = [
            jnp.where(here, jnp.where(lane - low == sub + SUB * g, 1.0, 0.0).astype(f32), plain[g])
            for g in pair
        ]
        upper = [jnp.zeros((SUB, LANES), f32)] * 2
        inverse = [jnp.zeros((SUB, LANES), f32)] * 2
        for first in range(0, 2 * SUB, 2):
            second = first + 1
            home, top, bottom = first // SUB, first % SUB, first % SUB + 1
            left, right = pivot[home][first], pivot[home][second]
            a, b, c = row_of(left, top), row_of(left, bottom), row_of(right, bottom)
            scale = 1.0 / (a * c - b * b)
            is_top, is_bottom = sub == top, sub == bottom
            both = is_top | is_bottom
            m_top, m_bottom = [], []
            for g in pair:
                p = pivot[g][first] * c - pivot[g][second] * b
                q = pivot[g][second] * a - pivot[g][first] * b
                if g == home:
                    p = jnp.where(is_top, -c, jnp.where(is_bottom, b, p))
                    q = jnp.where(is_top, b, jnp.where(is_bottom, -a, q))
                m_top.append(p * scale)
                m_bottom.append(q * scale)

            def eliminate(g, value, above, below):
                kept = jnp.where(both, 0.0, value) if g == home else value
                return kept - m_top[g] * above - m_bottom[g] * below

            w_top, w_bottom = row_of(work[home], top), row_of(work[home], bottom)
            p_top, p_bottom = row_of(plain[home], top), row_of(plain[home], bottom)
            root = lax.rsqrt(a)
            factor = b * root
            last = lax.rsqrt(c - factor * factor)
            upper[home] = jnp.where(
                is_top,
                p_top * root,
                jnp.where(is_bottom, (p_bottom - factor * (p_top * root)) * last, upper[home]),
            )
            inverse[home] = jnp.where(
                is_top,
                w_top * root,
                jnp.where(is_bottom, (w_bottom - factor * (w_top * root)) * last, inverse[home]),
            )
            for other in range(second + 1, 2 * SUB):
                above, below = row_of(pivot[home][other], top), row_of(pivot[home][other], bottom)
                for g in pair:
                    pivot[g][other] = eliminate(g, pivot[g][other], above, below)
            work = [eliminate(g, work[g], w_top, w_bottom) for g in pair]
            plain = [
                eliminate(g, plain[g], p_top, p_bottom) if g >= home else plain[g] for g in pair
            ]
        for g in pair:
            put(
                step + g,
                jnp.where(lane - low >= sub + SUB * g, upper[g], 0.0),
                jnp.where(lane - low <= sub + SUB * g, inverse[g], 0.0),
            )
        if step + 2 < number:
            solved = [row_of(work[c // SUB], c % SUB) for c in range(2 * SUB)]
            for i in range(step + 2, number):
                terms = [columns[i - step][c] * solved[c] for c in range(2 * SUB)]
                while len(terms) > 1:
                    terms = [terms[k] + terms[k + 1] for k in range(0, len(terms), 2)]
                rows[i] = jnp.where(here, 0.0, rows[i]) - terms[0]


def factor_block(rows, put):
    lane = lax.broadcasted_iota(jnp.int32, (SUB, LANES), 1)
    group = HALF // SUB
    for half in range(LANES // HALF):
        done = [None] * group

        def put_half(step, upper_rows, inverse_rows):
            put(group * half + step, upper_rows, inverse_rows)
            done[step] = jnp.where(lane < HALF * (half + 1), inverse_rows, upper_rows)

        chosen = rows[group * half : group * (half + 1)]
        factor_half(chosen, group * half, put_half)
        if half == 0:
            panel = jnp.concatenate(done, axis=0)
            change = mul(panel.T[HALF:], panel, NN, highest)
            for i in range(group):
                rows[group + i] = (
                    jnp.where(lane >= HALF, rows[group + i], 0.0) - change[SUB * i : SUB * (i + 1)]
                )


def factor_step(matrix, strip, corner, panel, k):
    size = matrix.shape[0]
    low, top = LANES * k, LANES * (k + 1)

    def put(step, upper_rows, inverse_rows):
        at = pl.ds(SUB * step, SUB)
        corner[at, :] = upper_rows
        panel[at, low:top] = inverse_rows

    factor_block(
        [matrix[low + SUB * i : low + SUB * (i + 1), low:top] for i in range(LANES // SUB)], put
    )
    own = panel[:, low:top]
    if low:
        strip[:low, :] = jnp.zeros((low, LANES), f32)
        panel[:, :low] = mul(own, matrix[low:top, :low], NN, highest)
        matrix[low:top, :low] = panel[:, :low]
    strip[low:top, :] = corner[...].T
    matrix[low:top, low:top] = own
    if top < size:
        panel[:, top:] = mul(own, matrix[low:top, top:], NN, highest)
        matrix[low:top, top:] = jnp.zeros((LANES, size - top), f32)
        for i in range(top, size, LANES):
            strip[i : i + LANES, :] = panel[:, i : i + LANES].T
        matrix[top:, low:top] = jnp.zeros((size - top, LANES), f32)
        matrix[top:, :] = matrix[top:, :] - mul(strip[top:, :], panel[...], NN, highest)


def kernel_tile(points):
    size = points.shape[1]
    spots = points.astype(f32)
    square = jnp.sum(spots * spots, axis=0, keepdims=True)
    one = jnp.ones_like(square)
    zero = jnp.zeros((11, size), f32)
    left = jnp.concatenate([spots, square, one, zero], axis=0).astype(bf16)
    right = jnp.concatenate([-2.0 * spots, one, square, zero], axis=0).astype(bf16)
    distance = mul(left, right, TN)
    row = lax.broadcasted_iota(jnp.int32, (size, size), 0)
    column = lax.broadcasted_iota(jnp.int32, (size, size), 1)
    return lax.rsqrt(distance + 1.0) * (1.0 / (4.0 * math.pi)) + jnp.where(row == column, 1.0, 0.0)


def onehot_rows(label_row):
    size = label_row.shape[1]
    row = lax.broadcasted_iota(jnp.int32, (NRHS, size), 0).astype(f32)
    return jnp.where(row == label_row, 1.0, 0.0).astype(f32)


def pack_kernel(ranks, labels, u, v, packed):
    size, breadth = u.shape
    position = lax.axis_index("row")
    lane = lax.broadcasted_iota(jnp.int32, (size, breadth), 1)
    own = position == 1
    packed[0:size, :] = jnp.where(own, u[...], 0).astype(bf16)
    packed[size : 2 * size, :] = jnp.where(own & (lane < ranks[0, 0]), v[...], 0).astype(bf16)
    spread = size // breadth
    label = jnp.concatenate(
        [labels[:, breadth * i : breadth * (i + 1)].astype(f32) for i in range(spread)] * 2
        + [jnp.zeros((16 - 2 * spread, breadth), f32)],
        axis=0,
    )
    row = lax.broadcasted_iota(jnp.int32, label.shape, 0)
    source = jnp.where(row < spread, 0, 1)
    packed[2 * size :, :] = jnp.where(source == position, label, 0.0).astype(bf16)


def first_kernel(k, *refs):
    if k == 0:
        coords, matrix, diagonal, strip, corner, panel, sem = refs
        matrix[...] = kernel_tile(coords[:, 0, :])
    else:
        old, _, matrix, diagonal, strip, corner, panel, sem = refs
        matrix[...] = old[...]
    factor_step(matrix, strip, corner, panel, k)
    copy = pltpu.make_async_copy(strip, diagonal.at[0, :, pl.ds(LANES * k, LANES)], sem)
    copy.start()
    copy.wait()


def second_kernel(
    coords, ranks, label_rows, got, came, inverse, u_first, v_first, u_second, v_second, _,
    diagonal, out,
    matrix, strip, corner, panel, y_first, y_second, z_first, z_second, result,
    u0, v0, u1, v1, in_sems, out_sems, strip_sems,
):
    size = inverse.shape[0]
    cycles = result.shape[0]
    loads = [
        pltpu.make_async_copy(source.at[:, 0], target, in_sems.at[i])
        for i, (source, target) in enumerate(
            ((u_first, u0), (v_first, v0), (u_second, u1), (v_second, v1))
        )
    ]
    for load in loads:
        load.start()
    shared = (got[...].astype(f32) + came[...].astype(f32))
    u_one = shared[0:size, :].astype(bf16)
    v_one = shared[size : 2 * size, :].astype(bf16)
    labels = shared[2 * size :, :]
    spread = size // LANES

    def label_row(which):
        return jnp.concatenate(
            [labels[which * spread + i : which * spread + i + 1, :] for i in range(spread)], axis=1
        )

    first_b = onehot_rows(label_row(0)).astype(bf16)
    y0 = split_left(inverse[...], first_b, NT)
    y_first[...] = y0
    w_one = split_left(inverse[...], v_one)
    gram = mul(w_one, w_one, TN, highest)
    left = split_right(u_one, gram)
    matrix[...] = kernel_tile(coords[:, 1, :]) - split_left(left, u_one, NT)
    target = onehot_rows(label_row(1)).T - split_right(u_one, mul(w_one, y0, TN, highest))
    z0 = mul(y0, inverse[...], TN, high)
    p_one = mul(inverse[...], w_one, TN, high)
    strips = []
    for k in range(size // LANES):
        factor_step(matrix, strip.at[k], corner, panel, k)
        copy = pltpu.make_async_copy(
            strip.at[k], diagonal.at[1, :, pl.ds(LANES * k, LANES)], strip_sems.at[k]
        )
        copy.start()
        strips.append(copy)
    y1 = mul(matrix[...], target, NN, high)
    y_second[...] = y1
    z1 = mul(y1, matrix[...], TN, high)
    q_one = split_left(z1, u_one, NN, 2)
    zc = z0 - mul(q_one, p_one, NT, high)
    for which, ref in ((zc, z_first), (z1, z_second)):
        big, small = parts_of(which, 2)
        ref[0:NRHS, :] = big
        ref[NRHS:, :] = small
    for load in loads:
        load.wait()
    columns = label_rows[:, 0, :].astype(f32).T
    lane = lax.broadcasted_iota(jnp.int32, (size, LANES), 1).astype(f32)
    keep = lax.broadcasted_iota(jnp.int32, (NRHS, LANES), 1)
    position = lax.axis_index("row")
    stores = []
    for at in range(0, cycles, 2):
        tiles = range(at, min(at + 2, cycles))

        def weights(v, z, which):
            both = mul(z[...], jnp.concatenate([v[t] for t in tiles], axis=1))
            value = both[:NRHS] + both[NRHS:]
            return [
                jnp.where(keep < ranks[which, t], value[:, LANES * i : LANES * (i + 1)], 0.0)
                for i, t in enumerate(tiles)
            ]

        h_first, h_second = weights(v0, z_first, 0), weights(v1, z_second, 1)
        for i, t in enumerate(tiles):
            both = jnp.concatenate([h_first[i], h_second[i]], axis=1)
            total = split_right(jnp.concatenate([u0[t], u1[t]], axis=1), both, NT, 2)
            column = jnp.broadcast_to(columns[:, t : t + 1], (size, LANES))
            hot = jnp.concatenate(
                [jnp.where(column == lane + float(LANES * j), 1.0, 0.0) for j in range(NRHS // LANES)],
                axis=1,
            )
            result[t] = hot - total
            if t == 0:

                @pl.when(position == 0)
                def _():
                    result[0] = y_first[...]

                @pl.when(position == 1)
                def _():
                    result[0] = y_second[...]

            store = pltpu.make_async_copy(result.at[t], out.at[t, 0], out_sems.at[t])
            store.start()
            stores.append(store)
    for copy in strips + stores:
        copy.wait()


def hops(number):
    chips = number // 2
    strides = [1 << b for b in range(max(chips - 1, 0).bit_length())]
    odd = strides[::-1]
    even = strides[:1] + strides[:0:-1]
    have = {0: [0], 1: [0]}
    result = []
    for index in range(len(strides)):
        pairs = []
        for core, order in ((1, odd), (0, even)):
            new = [(c, c ^ order[index]) for c in have[core] if c ^ order[index] < chips]
            pairs += [(2 * a + core, 2 * b + core) for a, b in new]
            have[core] = have[core] + [b for _, b in new]
        result.append(pairs)
    return result + [[(i, i ^ 1) for i in range(number)]]


def local(row_size, coords, labels, ranks, u_first, v_first, u_second, v_second):
    cycles, _, size, breadth = u_first.shape
    blocks = size // LANES
    whole = pl.BlockSpec(memory_space=VMEM)
    scalars = pl.BlockSpec(memory_space=pltpu.SMEM)
    anywhere = pl.BlockSpec(memory_space=pl.ANY)
    points = jnp.transpose(coords, (1, 0, 2))
    rank_rows = jnp.transpose(ranks, (1, 2, 0))[0]

    packed_size = 2 * size + 16

    def one(width):
        return pl.BlockSpec((None, None, size, width), lambda i: (0, 0, 0, 0))

    packed = pl.pallas_call(
        pack_kernel,
        out_shape=jax.ShapeDtypeStruct((packed_size, breadth), bf16),
        grid=(1,),
        in_specs=[scalars, pl.BlockSpec((None, 1, size), lambda i: (0, 0, 0)), one(breadth), one(breadth)],
        out_specs=pl.BlockSpec((packed_size, breadth), lambda i: (0, 0)),
        compiler_params=pltpu.CompilerParams(vmem_limit_bytes=8 << 20),
        name="pack",
    )(rank_rows, labels, u_first, v_first)

    square = jax.ShapeDtypeStruct((size, size), f32)
    stack = jax.ShapeDtypeStruct((2, size, size), f32)
    room = [
        pltpu.VMEM((LANES, LANES), f32),
        pltpu.VMEM((LANES, size), f32),
    ]
    state = (points,)
    for k in range(blocks):
        state = pl.pallas_call(
            functools.partial(first_kernel, k),
            out_shape=[square, stack],
            in_specs=[whole] if k == 0 else [whole, anywhere],
            out_specs=[whole, anywhere],
            input_output_aliases={} if k == 0 else {0: 0, 1: 1},
            scratch_shapes=[pltpu.VMEM((size, LANES), f32)] + room + [pltpu.SemaphoreType.DMA],
            compiler_params=pltpu.CompilerParams(vmem_limit_bytes=12 << 20),
            cost_estimate=pl.CostEstimate(flops=4 * 10**9, bytes_accessed=10**6, transcendentals=0),
            name=f"first{k}",
        )(*state)
    inverse, diagonal = state

    got = packed
    pairs = hops(row_size)
    for pair in pairs[:-1]:
        got = got + lax.ppermute(got, "row", pair)
    came = lax.ppermute(got, "row", pairs[-1])

    slab = pltpu.VMEM((cycles, size, breadth), bf16)
    diagonal, eliminated = pl.pallas_call(
        second_kernel,
        out_shape=[stack, jax.ShapeDtypeStruct((cycles, 1, size, NRHS), f32)],
        in_specs=[whole, scalars, whole, whole, whole, whole] + [anywhere] * 5,
        out_specs=[anywhere, anywhere],
        scratch_shapes=[
            pltpu.VMEM((size, size), f32),
            pltpu.VMEM((blocks, size, LANES), f32),
            *room,
            pltpu.VMEM((size, NRHS), f32),
            pltpu.VMEM((size, NRHS), f32),
            pltpu.VMEM((2 * NRHS, size), bf16),
            pltpu.VMEM((2 * NRHS, size), bf16),
            pltpu.VMEM((cycles, size, NRHS), f32),
            slab, slab, slab, slab,
            pltpu.SemaphoreType.DMA((4,)),
            pltpu.SemaphoreType.DMA((cycles,)),
            pltpu.SemaphoreType.DMA((blocks,)),
        ],
        input_output_aliases={10: 0},
        compiler_params=pltpu.CompilerParams(vmem_limit_bytes=40 << 20),
        name="second",
    )(
        points, rank_rows, labels, got, came, inverse,
        u_first, v_first, u_second, v_second, diagonal,
    )
    return (eliminated, diagonal)


def solution(mesh):
    in_specs = (
        P("parts", None, None),
        P("parts", "row", None),
        P("parts", "row", None),
        P("parts", "row", None, None),
        P("parts", "row", None, None),
        P("parts", "row", None, None),
        P("parts", "row", None, None),
    )
    out_specs = (P("parts", "row", None, None), P("parts", None, None))
    return jax.shard_map(
        functools.partial(local, mesh.shape["row"]),
        mesh=mesh, in_specs=in_specs, out_specs=out_specs, check_vma=False,
    )
```

```python
import functools
import math

import jax
import jax.numpy as jnp
from jax import lax
from jax.experimental import pallas as pl
from jax.experimental.pallas import tpu as pltpu
from jax.sharding import PartitionSpec as P

NRHS = 256
LANES = 128
SUB = 8
HALF = 64
f32 = jnp.float32
bf16 = jnp.bfloat16
highest = lax.Precision.HIGHEST
high = lax.Precision.HIGH
VMEM = pltpu.VMEM
NN, TN, NT = ((1,), (0,)), ((0,), (0,)), ((1,), (1,))


def mul(left, right, dims=NN, precision=None):
    return lax.dot_general(
        left, right, (dims, ((), ())), precision=precision, preferred_element_type=f32
    )


def parts_of(value, number):
    pieces = []
    for _ in range(number):
        piece = value.astype(bf16)
        pieces.append(piece)
        value = value - piece.astype(f32)
    return pieces


def split_left(left, right, dims=NN, number=3):
    return sum(mul(piece, right, dims) for piece in reversed(parts_of(left, number)))


def split_right(left, right, dims=NN, number=3):
    return sum(mul(left, piece, dims) for piece in reversed(parts_of(right, number)))


def lower_left(product, lower, right):
    size = lower.shape[0]
    half = size // 2
    return jnp.concatenate(
        [product(lower[:half, :half], right[:half]), product(lower[half:, :], right)], axis=0
    )


def lower_right(left, lower):
    half = lower.shape[0] // 2
    return jnp.concatenate(
        [mul(left, lower[:, :half], TN, high), mul(left[half:], lower[half:, half:], TN, high)], axis=1
    )


def row_of(value, index):
    return jnp.broadcast_to(value[index : index + 1, :], value.shape)


def column_of(value, index):
    return jnp.broadcast_to(value[:, index : index + 1], value.shape)


def factor_half(rows, base, put):
    number = len(rows)
    lane = lax.broadcasted_iota(jnp.int32, (SUB, LANES), 1)
    sub = lax.broadcasted_iota(jnp.int32, (SUB, LANES), 0)
    pair = range(2)
    for step in range(0, number, 2):
        low = SUB * (base + step)
        here = (lane >= low) & (lane < low + 2 * SUB)
        columns = [[column_of(rows[i], low + c) for c in range(2 * SUB)] for i in range(step, number)]
        pivot = [list(columns[0]), list(columns[1])]
        plain = [rows[step], rows[step + 1]]
        work = [
            jnp.where(here, jnp.where(lane - low == sub + SUB * g, 1.0, 0.0).astype(f32), plain[g])
            for g in pair
        ]
        upper = [jnp.zeros((SUB, LANES), f32)] * 2
        inverse = [jnp.zeros((SUB, LANES), f32)] * 2
        for first in range(0, 2 * SUB, 2):
            second = first + 1
            home, top, bottom = first // SUB, first % SUB, first % SUB + 1
            left, right = pivot[home][first], pivot[home][second]
            a, b, c = row_of(left, top), row_of(left, bottom), row_of(right, bottom)
            scale = 1.0 / (a * c - b * b)
            is_top, is_bottom = sub == top, sub == bottom
            both = is_top | is_bottom
            m_top, m_bottom = [], []
            for g in pair:
                p = pivot[g][first] * c - pivot[g][second] * b
                q = pivot[g][second] * a - pivot[g][first] * b
                if g == home:
                    p = jnp.where(is_top, -c, jnp.where(is_bottom, b, p))
                    q = jnp.where(is_top, b, jnp.where(is_bottom, -a, q))
                m_top.append(p * scale)
                m_bottom.append(q * scale)

            def eliminate(g, value, above, below):
                kept = jnp.where(both, 0.0, value) if g == home else value
                return kept - m_top[g] * above - m_bottom[g] * below

            w_top, w_bottom = row_of(work[home], top), row_of(work[home], bottom)
            p_top, p_bottom = row_of(plain[home], top), row_of(plain[home], bottom)
            root = lax.rsqrt(a)
            factor = b * root
            last = lax.rsqrt(c - factor * factor)
            upper[home] = jnp.where(
                is_top,
                p_top * root,
                jnp.where(is_bottom, (p_bottom - factor * (p_top * root)) * last, upper[home]),
            )
            inverse[home] = jnp.where(
                is_top,
                w_top * root,
                jnp.where(is_bottom, (w_bottom - factor * (w_top * root)) * last, inverse[home]),
            )
            for other in range(second + 1, 2 * SUB):
                above, below = row_of(pivot[home][other], top), row_of(pivot[home][other], bottom)
                for g in pair:
                    pivot[g][other] = eliminate(g, pivot[g][other], above, below)
            work = [eliminate(g, work[g], w_top, w_bottom) for g in pair]
            plain = [
                eliminate(g, plain[g], p_top, p_bottom) if g >= home else plain[g] for g in pair
            ]
        for g in pair:
            put(
                step + g,
                jnp.where(lane - low >= sub + SUB * g, upper[g], 0.0),
                jnp.where(lane - low <= sub + SUB * g, inverse[g], 0.0),
            )
        if step + 2 < number:
            solved = [row_of(work[c // SUB], c % SUB) for c in range(2 * SUB)]
            for i in range(step + 2, number):
                terms = [columns[i - step][c] * solved[c] for c in range(2 * SUB)]
                while len(terms) > 1:
                    terms = [terms[k] + terms[k + 1] for k in range(0, len(terms), 2)]
                rows[i] = jnp.where(here, 0.0, rows[i]) - terms[0]


def factor_block(rows, put):
    lane = lax.broadcasted_iota(jnp.int32, (SUB, LANES), 1)
    group = HALF // SUB
    for half in range(LANES // HALF):
        done = [None] * group

        def put_half(step, upper_rows, inverse_rows):
            put(group * half + step, upper_rows, inverse_rows)
            done[step] = jnp.where(lane < HALF * (half + 1), inverse_rows, upper_rows)

        chosen = rows[group * half : group * (half + 1)]
        factor_half(chosen, group * half, put_half)
        if half == 0:
            panel = jnp.concatenate(done, axis=0)
            change = mul(panel.T[HALF:], panel, NN, highest)
            for i in range(group):
                rows[group + i] = (
                    jnp.where(lane >= HALF, rows[group + i], 0.0) - change[SUB * i : SUB * (i + 1)]
                )


def factor_step(matrix, strip, corner, panel, k):
    size = matrix.shape[0]
    low, top = LANES * k, LANES * (k + 1)

    def put(step, upper_rows, inverse_rows):
        at = pl.ds(SUB * step, SUB)
        corner[at, :] = upper_rows
        panel[at, low:top] = inverse_rows

    factor_block(
        [matrix[low + SUB * i : low + SUB * (i + 1), low:top] for i in range(LANES // SUB)], put
    )
    own = panel[:, low:top]
    if low:
        strip[:low, :] = jnp.zeros((low, LANES), f32)
        panel[:, :low] = mul(own, matrix[low:top, :low], NN, highest)
        matrix[low:top, :low] = panel[:, :low]
    strip[low:top, :] = corner[...].T
    matrix[low:top, low:top] = own
    if top < size:
        panel[:, top:] = mul(own, matrix[low:top, top:], NN, highest)
        matrix[low:top, top:] = jnp.zeros((LANES, size - top), f32)
        for i in range(top, size, LANES):
            strip[i : i + LANES, :] = panel[:, i : i + LANES].T
        matrix[top:, low:top] = jnp.zeros((size - top, LANES), f32)
        matrix[top:, :] = matrix[top:, :] - mul(strip[top:, :], panel[...], NN, highest)


def kernel_tile(points):
    size = points.shape[1]
    spots = points.astype(f32)
    square = jnp.sum(spots * spots, axis=0, keepdims=True)
    one = jnp.ones_like(square)
    zero = jnp.zeros((11, size), f32)
    left = jnp.concatenate([spots, square, one, zero], axis=0).astype(bf16)
    right = jnp.concatenate([-2.0 * spots, one, square, zero], axis=0).astype(bf16)
    distance = mul(left, right, TN)
    row = lax.broadcasted_iota(jnp.int32, (size, size), 0)
    column = lax.broadcasted_iota(jnp.int32, (size, size), 1)
    return lax.rsqrt(distance + 1.0) * (1.0 / (4.0 * math.pi)) + jnp.where(row == column, 1.0, 0.0)


def onehot_rows(label_row):
    size = label_row.shape[1]
    row = lax.broadcasted_iota(jnp.int32, (NRHS, size), 0).astype(f32)
    return jnp.where(row == label_row, 1.0, 0.0).astype(f32)


def pack(ranks, labels, u, v, packed):
    size, breadth = u.shape
    position = lax.axis_index("row")
    lane = lax.broadcasted_iota(jnp.int32, (size, breadth), 1)
    own = position == 1
    packed[0:size, :] = jnp.where(own, u[...], 0).astype(bf16)
    packed[size : 2 * size, :] = jnp.where(own & (lane < ranks[0, 0]), v[...], 0).astype(bf16)
    spread = size // breadth
    label = jnp.concatenate(
        [labels[:, breadth * i : breadth * (i + 1)].astype(f32) for i in range(spread)] * 2
        + [jnp.zeros((16 - 2 * spread, breadth), f32)],
        axis=0,
    )
    row = lax.broadcasted_iota(jnp.int32, label.shape, 0)
    source = jnp.where(row < spread, 0, 1)
    packed[2 * size :, :] = jnp.where(source == position, label, 0.0).astype(bf16)


def first_kernel(
    coords, ranks, labels, u_first, v_first,
    matrix, diagonal, packed,
    strip, corner, panel, points, rank_rows, label_row, u_one, v_one, sem, sems,
):
    loads = [
        pltpu.make_async_copy(source, target, sems.at[i])
        for i, (source, target) in enumerate(
            (
                (coords, points),
                (u_first.at[0, 0], u_one),
                (v_first.at[0, 0], v_one),
                (labels.at[0], label_row),
                (ranks, rank_rows),
            )
        )
    ]
    for load in loads:
        load.start()
    loads[0].wait()
    matrix[...] = kernel_tile(points[:, 0, :])
    for load in loads[1:]:
        load.wait()
    pack(rank_rows, label_row, u_one, v_one, packed)
    first_step(0, matrix, diagonal, strip, corner, panel, sem)


def next_kernel(k, old, _, matrix, diagonal, strip, corner, panel, sem):
    matrix[...] = old[...]
    first_step(k, matrix, diagonal, strip, corner, panel, sem)


def first_step(k, matrix, diagonal, strip, corner, panel, sem):
    factor_step(matrix, strip, corner, panel, k)
    copy = pltpu.make_async_copy(strip, diagonal.at[0, :, pl.ds(LANES * k, LANES)], sem)
    copy.start()
    copy.wait()


def second_kernel(
    coords, ranks, label_rows, got, came, inverse, u0, v0, u1, v1, _,
    diagonal, out,
    matrix, strip, corner, panel, y_first, y_second, z_first, z_second, result,
    out_sems, strip_sems,
):
    size = inverse.shape[0]
    cycles = result.shape[0]
    shared = (got[...].astype(f32) + came[...].astype(f32))
    u_one = shared[0:size, :].astype(bf16)
    v_one = shared[size : 2 * size, :].astype(bf16)
    labels = shared[2 * size :, :]
    spread = size // LANES

    def label_row(which):
        return jnp.concatenate(
            [labels[which * spread + i : which * spread + i + 1, :] for i in range(spread)], axis=1
        )

    first_b = onehot_rows(label_row(0)).astype(bf16)
    y0 = split_left(inverse[...], first_b, NT)
    y_first[...] = y0
    w_one = lower_left(split_left, inverse[...], v_one)
    gram = mul(w_one, w_one, TN, highest)
    left = split_right(u_one, gram)
    matrix[...] = kernel_tile(coords[:, 1, :]) - split_left(left, u_one, NT)
    target = onehot_rows(label_row(1)).T - split_right(u_one, mul(w_one, y0, TN, highest))
    z0 = lower_right(y0, inverse[...])
    p_one = mul(inverse[...], w_one, TN, high)
    strips = []
    for k in range(size // LANES):
        factor_step(matrix, strip.at[k], corner, panel, k)
        copy = pltpu.make_async_copy(
            strip.at[k], diagonal.at[1, :, pl.ds(LANES * k, LANES)], strip_sems.at[k]
        )
        copy.start()
        strips.append(copy)
    y1 = lower_left(functools.partial(mul, precision=high), matrix[...], target)
    y_second[...] = y1
    z1 = lower_right(y1, matrix[...])
    q_one = split_left(z1, u_one, NN, 2)
    zc = z0 - mul(q_one, p_one, NT, high)
    for which, ref in ((zc, z_first), (z1, z_second)):
        big, small = parts_of(which, 2)
        ref[0:NRHS, :] = big
        ref[NRHS:, :] = small
    columns = label_rows[:, 0, :].astype(f32).T
    lane = lax.broadcasted_iota(jnp.int32, (size, LANES), 1).astype(f32)
    keep = lax.broadcasted_iota(jnp.int32, (NRHS, LANES), 1)
    position = lax.axis_index("row")
    stores = []
    for at in range(0, cycles, 2):
        tiles = range(at, min(at + 2, cycles))

        def weights(v, z, which):
            both = mul(z[...], jnp.concatenate([v[t, 0] for t in tiles], axis=1))
            value = both[:NRHS] + both[NRHS:]
            return [
                jnp.where(keep < ranks[which, t], value[:, LANES * i : LANES * (i + 1)], 0.0)
                for i, t in enumerate(tiles)
            ]

        h_first, h_second = weights(v0, z_first, 0), weights(v1, z_second, 1)
        for i, t in enumerate(tiles):
            both = jnp.concatenate([h_first[i], h_second[i]], axis=1)
            total = split_right(jnp.concatenate([u0[t, 0], u1[t, 0]], axis=1), both, NT, 2)
            column = jnp.broadcast_to(columns[:, t : t + 1], (size, LANES))
            hot = jnp.concatenate(
                [jnp.where(column == lane + float(LANES * j), 1.0, 0.0) for j in range(NRHS // LANES)],
                axis=1,
            )
            result[t] = hot - total
            if t == 0:

                @pl.when(position == 0)
                def _():
                    result[0] = y_first[...]

                @pl.when(position == 1)
                def _():
                    result[0] = y_second[...]

            store = pltpu.make_async_copy(result.at[t], out.at[t, 0], out_sems.at[t])
            store.start()
            stores.append(store)
    for copy in strips + stores:
        copy.wait()


def hops(number):
    chips = number // 2
    strides = [1 << b for b in range(max(chips - 1, 0).bit_length())]
    odd = strides[::-1]
    even = strides[:1] + strides[:0:-1]
    have = {0: [0], 1: [0]}
    result = []
    for index in range(len(strides)):
        pairs = []
        for core, order in ((1, odd), (0, even)):
            new = [(c, c ^ order[index]) for c in have[core] if c ^ order[index] < chips]
            pairs += [(2 * a + core, 2 * b + core) for a, b in new]
            have[core] = have[core] + [b for _, b in new]
        result.append(pairs)
    return result + [[(i, i ^ 1) for i in range(number)]]


def local(row_size, coords, labels, ranks, u_first, v_first, u_second, v_second):
    cycles, _, size, breadth = u_first.shape
    blocks = size // LANES
    whole = pl.BlockSpec(memory_space=VMEM)
    scalars = pl.BlockSpec(memory_space=pltpu.SMEM)
    anywhere = pl.BlockSpec(memory_space=pl.ANY)
    points = jnp.transpose(coords, (1, 0, 2))
    rank_rows = jnp.transpose(ranks, (1, 2, 0))[0]

    packed_size = 2 * size + 16

    square = jax.ShapeDtypeStruct((size, size), f32)
    stack = jax.ShapeDtypeStruct((2, size, size), f32)
    room = [
        pltpu.VMEM((LANES, LANES), f32),
        pltpu.VMEM((LANES, size), f32),
    ]
    params = pltpu.CompilerParams(vmem_limit_bytes=12 << 20)
    estimate = pl.CostEstimate(flops=4 * 10**9, bytes_accessed=10**6, transcendentals=0)
    strip = [pltpu.VMEM((size, LANES), f32)]
    inverse, diagonal, packed = pl.pallas_call(
        first_kernel,
        out_shape=[square, stack, jax.ShapeDtypeStruct((packed_size, breadth), bf16)],
        in_specs=[pl.BlockSpec(memory_space=pltpu.HBM)] * 5,
        out_specs=[whole, anywhere, whole],
        scratch_shapes=strip
        + room
        + [
            pltpu.VMEM(points.shape, jnp.int32),
            pltpu.SMEM(rank_rows.shape, jnp.int32),
            pltpu.VMEM((1, size), jnp.int32),
            pltpu.VMEM((size, breadth), bf16),
            pltpu.VMEM((size, breadth), bf16),
            pltpu.SemaphoreType.DMA,
            pltpu.SemaphoreType.DMA((5,)),
        ],
        compiler_params=params,
        cost_estimate=estimate,
        name="first0",
    )(*(pltpu.with_memory_space_constraint(x, pltpu.HBM) for x in (points, rank_rows, labels, u_first, v_first)))
    got = packed
    pairs = hops(row_size)
    for k in range(1, blocks):
        late = lax.ppermute(got, "row", pairs[k - 1]) if k < len(pairs) else None
        inverse, diagonal = pl.pallas_call(
            functools.partial(next_kernel, k),
            out_shape=[square, stack],
            in_specs=[whole, anywhere],
            out_specs=[whole, anywhere],
            input_output_aliases={0: 0, 1: 1},
            scratch_shapes=strip + room + [pltpu.SemaphoreType.DMA],
            compiler_params=params,
            cost_estimate=estimate,
            name=f"first{k}",
        )(inverse, diagonal)
        if late is not None:
            late, inverse = lax.optimization_barrier((late, inverse))
            got = got + late

    for pair in pairs[blocks - 1 : -1]:
        got = got + lax.ppermute(got, "row", pair)
    came = lax.ppermute(got, "row", pairs[-1])

    diagonal, eliminated = pl.pallas_call(
        second_kernel,
        out_shape=[stack, jax.ShapeDtypeStruct((cycles, 1, size, NRHS), f32)],
        in_specs=[whole, scalars] + [whole] * 8 + [anywhere],
        out_specs=[anywhere, anywhere],
        scratch_shapes=[
            pltpu.VMEM((size, size), f32),
            pltpu.VMEM((blocks, size, LANES), f32),
            *room,
            pltpu.VMEM((size, NRHS), f32),
            pltpu.VMEM((size, NRHS), f32),
            pltpu.VMEM((2 * NRHS, size), bf16),
            pltpu.VMEM((2 * NRHS, size), bf16),
            pltpu.VMEM((cycles, size, NRHS), f32),
            pltpu.SemaphoreType.DMA((cycles,)),
            pltpu.SemaphoreType.DMA((blocks,)),
        ],
        input_output_aliases={10: 0},
        compiler_params=pltpu.CompilerParams(vmem_limit_bytes=40 << 20),
        name="second",
    )(
        points, rank_rows, labels, got, came, inverse,
        u_first, v_first, u_second, v_second, diagonal,
    )
    return (eliminated, diagonal)


def solution(mesh):
    in_specs = (
        P("parts", None, None),
        P("parts", "row", None),
        P("parts", "row", None),
        P("parts", "row", None, None),
        P("parts", "row", None, None),
        P("parts", "row", None, None),
        P("parts", "row", None, None),
    )
    out_specs = (P("parts", "row", None, None), P("parts", None, None))
    return jax.shard_map(
        functools.partial(local, mesh.shape["row"]),
        mesh=mesh, in_specs=in_specs, out_specs=out_specs, check_vma=False,
    )
```

```python
import functools
import math

import jax
import jax.numpy as jnp
from jax import lax
from jax.experimental import pallas as pl
from jax.experimental.pallas import tpu as pltpu
from jax.sharding import PartitionSpec as P

NRHS = 256
LANES = 128
SUB = 8
f32 = jnp.float32
bf16 = jnp.bfloat16
highest = lax.Precision.HIGHEST
high = lax.Precision.HIGH
VMEM = pltpu.VMEM
NN, TN, NT = ((1,), (0,)), ((0,), (0,)), ((1,), (1,))


def mul(left, right, dims=NN, precision=None):
    return lax.dot_general(
        left, right, (dims, ((), ())), precision=precision, preferred_element_type=f32
    )


def parts_of(value, number):
    pieces = []
    for _ in range(number):
        piece = value.astype(bf16)
        pieces.append(piece)
        value = value - piece.astype(f32)
    return pieces


def split_left(left, right, dims=NN, number=3):
    return sum(mul(piece, right, dims) for piece in reversed(parts_of(left, number)))


def split_right(left, right, dims=NN, number=3):
    return sum(mul(left, piece, dims) for piece in reversed(parts_of(right, number)))


def lower_left(product, lower, right):
    size = lower.shape[0]
    half = size // 2
    return jnp.concatenate(
        [product(lower[:half, :half], right[:half]), product(lower[half:, :], right)], axis=0
    )


def lower_right(left, lower):
    half = lower.shape[0] // 2
    return jnp.concatenate(
        [mul(left, lower[:, :half], TN, high), mul(left[half:], lower[half:, half:], TN, high)], axis=1
    )


def row_of(value, index):
    return jnp.broadcast_to(value[index : index + 1, :], value.shape)


def column_of(value, index):
    return jnp.broadcast_to(value[:, index : index + 1], value.shape)


def tree_sum(terms):
    while len(terms) > 1:
        terms = [terms[k] + terms[k + 1] for k in range(0, len(terms), 2)]
    return terms[0]


def factor_block(rows, put):
    number = len(rows)
    lane = lax.broadcasted_iota(jnp.int32, (SUB, LANES), 1)
    sub = lax.broadcasted_iota(jnp.int32, (SUB, LANES), 0)
    pair = range(2)
    zero = jnp.zeros((SUB, LANES), f32)
    for step in range(0, number, 2):
        low = SUB * step
        here = (lane >= low) & (lane < low + 2 * SUB)
        far = step + 4
        columns = [
            [column_of(rows[i], low + c) for c in range(2 * SUB)]
            for i in range(step, min(number, far))
        ]
        pivot = [list(columns[0]), list(columns[1])]
        plain = [rows[step], rows[step + 1]]
        work = [
            jnp.where(here, jnp.where(lane - low == sub + SUB * g, 1.0, 0.0).astype(f32), plain[g])
            for g in pair
        ]
        upper, inverse, roots = [zero] * 2, [zero] * 2, [zero] * 2
        for first in range(0, 2 * SUB, 2):
            second = first + 1
            home, top, bottom = first // SUB, first % SUB, first % SUB + 1
            left, right = pivot[home][first], pivot[home][second]
            a, b, c = row_of(left, top), row_of(left, bottom), row_of(right, bottom)
            det = a * c - b * b
            scale = 1.0 / det
            is_top, is_bottom = sub == top, sub == bottom
            m_top, m_bottom = {}, {}
            for g in pair[home:]:
                p = pivot[g][first] * c - pivot[g][second] * b
                q = pivot[g][second] * a - pivot[g][first] * b
                if g == home:
                    p = jnp.where(is_top, det - c, jnp.where(is_bottom, b, p))
                    q = jnp.where(is_top, b, jnp.where(is_bottom, det - a, q))
                m_top[g], m_bottom[g] = p * scale, q * scale

            def eliminate(g, value, above, below):
                return value - m_top[g] * above - m_bottom[g] * below

            w_top, w_bottom = row_of(work[home], top), row_of(work[home], bottom)
            p_top, p_bottom = row_of(plain[home], top), row_of(plain[home], bottom)
            ratio = b * (1.0 / a)
            after = sub >= top
            upper[home] = jnp.where(
                after, jnp.where(is_top, p_top, p_bottom - ratio * p_top), upper[home]
            )
            inverse[home] = jnp.where(
                after, jnp.where(is_top, w_top, w_bottom - ratio * w_top), inverse[home]
            )
            roots[home] = jnp.where(
                after, jnp.where(is_top, lax.rsqrt(a), lax.rsqrt(c - b * ratio)), roots[home]
            )
            for other in range(second + 1, 2 * SUB):
                above, below = row_of(pivot[home][other], top), row_of(pivot[home][other], bottom)
                for g in pair[home:]:
                    pivot[g][other] = eliminate(g, pivot[g][other], above, below)
            for g in pair[home:]:
                work[g] = eliminate(g, work[g], w_top, w_bottom)
                plain[g] = eliminate(g, plain[g], p_top, p_bottom)
        for g in pair:
            put(
                step + g,
                jnp.where(lane - low >= sub + SUB * g, upper[g] * roots[g], 0.0),
                jnp.where(lane - low <= sub + SUB * g, inverse[g] * roots[g], 0.0),
            )
        if step + 2 < number:
            solved = [row_of(work[1], c) for c in range(SUB)]
            work[0] = work[0] - tree_sum([pivot[0][SUB + c] * solved[c] for c in range(SUB)])
            solved = [row_of(work[0], c) for c in range(SUB)] + solved
            if far < number:
                spread = jnp.concatenate([zero] * step + work + [zero] * (number - 2 - step), axis=0)
                change = mul(jnp.concatenate(rows[far:], axis=0), spread, NN, highest)
            for i in range(step + 2, number):
                if i < far:
                    update = tree_sum([columns[i - step][c] * solved[c] for c in range(2 * SUB)])
                else:
                    update = change[SUB * (i - far) : SUB * (i - far + 1)]
                rows[i] = jnp.where(here, 0.0, rows[i]) - update


def factor_step(matrix, strip, corner, panel, k):
    size = matrix.shape[0]
    low, top = LANES * k, LANES * (k + 1)

    def put(step, upper_rows, inverse_rows):
        at = pl.ds(SUB * step, SUB)
        corner[at, :] = upper_rows
        panel[at, low:top] = inverse_rows

    factor_block(
        [matrix[low + SUB * i : low + SUB * (i + 1), low:top] for i in range(LANES // SUB)], put
    )
    own = panel[:, low:top]
    if low:
        strip[:low, :] = jnp.zeros((low, LANES), f32)
        panel[:, :low] = mul(own, matrix[low:top, :low], NN, highest)
        matrix[low:top, :low] = panel[:, :low]
    strip[low:top, :] = corner[...].T
    matrix[low:top, low:top] = own
    if top < size:
        panel[:, top:] = mul(own, matrix[low:top, top:], NN, highest)
        matrix[low:top, top:] = jnp.zeros((LANES, size - top), f32)
        for i in range(top, size, LANES):
            strip[i : i + LANES, :] = panel[:, i : i + LANES].T
        matrix[top:, low:top] = jnp.zeros((size - top, LANES), f32)
        matrix[top:, :] = matrix[top:, :] - mul(strip[top:, :], panel[...], NN, highest)


def kernel_tile(points):
    size = points.shape[1]
    spots = points.astype(f32)
    square = jnp.sum(spots * spots, axis=0, keepdims=True)
    one = jnp.ones_like(square)
    zero = jnp.zeros((11, size), f32)
    left = jnp.concatenate([spots, square, one, zero], axis=0).astype(bf16)
    right = jnp.concatenate([-2.0 * spots, one, square, zero], axis=0).astype(bf16)
    distance = mul(left, right, TN)
    row = lax.broadcasted_iota(jnp.int32, (size, size), 0)
    column = lax.broadcasted_iota(jnp.int32, (size, size), 1)
    return lax.rsqrt(distance + 1.0) * (1.0 / (4.0 * math.pi)) + jnp.where(row == column, 1.0, 0.0)


def onehot_rows(label_row):
    size = label_row.shape[1]
    row = lax.broadcasted_iota(jnp.int32, (NRHS, size), 0).astype(f32)
    return jnp.where(row == label_row, 1.0, 0.0).astype(f32)


def pack(ranks, labels, u, v, packed):
    size, breadth = u.shape
    position = lax.axis_index("row")
    lane = lax.broadcasted_iota(jnp.int32, (size, breadth), 1)
    own = position == 1
    packed[0:size, :] = jnp.where(own, u[...], 0).astype(bf16)
    packed[size : 2 * size, :] = jnp.where(own & (lane < ranks[0, 0]), v[...], 0).astype(bf16)
    spread = size // breadth
    label = jnp.concatenate(
        [labels[:, breadth * i : breadth * (i + 1)].astype(f32) for i in range(spread)] * 2
        + [jnp.zeros((16 - 2 * spread, breadth), f32)],
        axis=0,
    )
    row = lax.broadcasted_iota(jnp.int32, label.shape, 0)
    source = jnp.where(row < spread, 0, 1)
    packed[2 * size :, :] = jnp.where(source == position, label, 0.0).astype(bf16)


def first_kernel(
    coords, ranks, labels, u_first, v_first,
    matrix, diagonal, packed,
    strip, corner, panel, points, rank_rows, label_row, u_one, v_one, sem, sems,
):
    loads = [
        pltpu.make_async_copy(source, target, sems.at[i])
        for i, (source, target) in enumerate(
            (
                (coords, points),
                (u_first.at[0, 0], u_one),
                (v_first.at[0, 0], v_one),
                (labels.at[0], label_row),
                (ranks, rank_rows),
            )
        )
    ]
    for load in loads:
        load.start()
    loads[0].wait()
    matrix[...] = kernel_tile(points[:, 0, :])
    for load in loads[1:]:
        load.wait()
    pack(rank_rows, label_row, u_one, v_one, packed)
    first_step(0, matrix, diagonal, strip, corner, panel, sem)


def next_kernel(k, old, _, matrix, diagonal, strip, corner, panel, sem):
    matrix[...] = old[...]
    first_step(k, matrix, diagonal, strip, corner, panel, sem)


def first_step(k, matrix, diagonal, strip, corner, panel, sem):
    factor_step(matrix, strip, corner, panel, k)
    copy = pltpu.make_async_copy(strip, diagonal.at[0, :, pl.ds(LANES * k, LANES)], sem)
    copy.start()
    copy.wait()


def second_kernel(
    coords, ranks, label_rows, got, came, inverse, u0, v0, u1, v1, _,
    diagonal, out,
    matrix, strip, corner, panel, y_first, y_second, z_first, z_second, result,
    out_sems, strip_sems,
):
    size = inverse.shape[0]
    cycles = result.shape[0]
    shared = (got[...].astype(f32) + came[...].astype(f32))
    u_one = shared[0:size, :].astype(bf16)
    v_one = shared[size : 2 * size, :].astype(bf16)
    labels = shared[2 * size :, :]
    spread = size // LANES

    def label_row(which):
        return jnp.concatenate(
            [labels[which * spread + i : which * spread + i + 1, :] for i in range(spread)], axis=1
        )

    first_b = onehot_rows(label_row(0)).astype(bf16)
    y0 = split_left(inverse[...], first_b, NT)
    y_first[...] = y0
    w_one = lower_left(split_left, inverse[...], v_one)
    gram = mul(w_one, w_one, TN, highest)
    left = split_right(u_one, gram)
    matrix[...] = kernel_tile(coords[:, 1, :]) - split_left(left, u_one, NT)
    target = onehot_rows(label_row(1)).T - split_right(u_one, mul(w_one, y0, TN, highest))
    z0 = lower_right(y0, inverse[...])
    p_one = mul(inverse[...], w_one, TN, high)
    strips = []
    for k in range(size // LANES):
        factor_step(matrix, strip.at[k], corner, panel, k)
        copy = pltpu.make_async_copy(
            strip.at[k], diagonal.at[1, :, pl.ds(LANES * k, LANES)], strip_sems.at[k]
        )
        copy.start()
        strips.append(copy)
    y1 = lower_left(functools.partial(mul, precision=high), matrix[...], target)
    y_second[...] = y1
    z1 = lower_right(y1, matrix[...])
    q_one = split_left(z1, u_one, NN, 2)
    zc = z0 - mul(q_one, p_one, NT, high)
    for which, ref in ((zc, z_first), (z1, z_second)):
        big, small = parts_of(which, 2)
        ref[0:NRHS, :] = big
        ref[NRHS:, :] = small
    columns = label_rows[:, 0, :].astype(f32).T
    lane = lax.broadcasted_iota(jnp.int32, (size, LANES), 1).astype(f32)
    keep = lax.broadcasted_iota(jnp.int32, (NRHS, LANES), 1)
    position = lax.axis_index("row")
    stores = []
    for at in range(0, cycles, 2):
        tiles = range(at, min(at + 2, cycles))

        def weights(v, z, which):
            both = mul(z[...], jnp.concatenate([v[t, 0] for t in tiles], axis=1))
            value = both[:NRHS] + both[NRHS:]
            return [
                jnp.where(keep < ranks[which, t], value[:, LANES * i : LANES * (i + 1)], 0.0)
                for i, t in enumerate(tiles)
            ]

        h_first, h_second = weights(v0, z_first, 0), weights(v1, z_second, 1)
        for i, t in enumerate(tiles):
            both = jnp.concatenate([h_first[i], h_second[i]], axis=1)
            total = split_right(jnp.concatenate([u0[t, 0], u1[t, 0]], axis=1), both, NT, 2)
            column = jnp.broadcast_to(columns[:, t : t + 1], (size, LANES))
            hot = jnp.concatenate(
                [jnp.where(column == lane + float(LANES * j), 1.0, 0.0) for j in range(NRHS // LANES)],
                axis=1,
            )
            result[t] = hot - total
            if t == 0:

                @pl.when(position == 0)
                def _():
                    result[0] = y_first[...]

                @pl.when(position == 1)
                def _():
                    result[0] = y_second[...]

            store = pltpu.make_async_copy(result.at[t], out.at[t, 0], out_sems.at[t])
            store.start()
            stores.append(store)
    for copy in strips + stores:
        copy.wait()


def hops(number):
    chips = number // 2
    strides = [1 << b for b in range(max(chips - 1, 0).bit_length())]
    odd = strides[::-1]
    even = strides[:1] + strides[:0:-1]
    have = {0: [0], 1: [0]}
    result = []
    for index in range(len(strides)):
        pairs = []
        for core, order in ((1, odd), (0, even)):
            new = [(c, c ^ order[index]) for c in have[core] if c ^ order[index] < chips]
            pairs += [(2 * a + core, 2 * b + core) for a, b in new]
            have[core] = have[core] + [b for _, b in new]
        result.append(pairs)
    return result + [[(i, i ^ 1) for i in range(number)]]


def local(row_size, coords, labels, ranks, u_first, v_first, u_second, v_second):
    cycles, _, size, breadth = u_first.shape
    blocks = size // LANES
    whole = pl.BlockSpec(memory_space=VMEM)
    scalars = pl.BlockSpec(memory_space=pltpu.SMEM)
    anywhere = pl.BlockSpec(memory_space=pl.ANY)
    points = jnp.transpose(coords, (1, 0, 2))
    rank_rows = jnp.transpose(ranks, (1, 2, 0))[0]

    packed_size = 2 * size + 16

    square = jax.ShapeDtypeStruct((size, size), f32)
    stack = jax.ShapeDtypeStruct((2, size, size), f32)
    room = [
        pltpu.VMEM((LANES, LANES), f32),
        pltpu.VMEM((LANES, size), f32),
    ]
    params = pltpu.CompilerParams(vmem_limit_bytes=12 << 20)
    estimate = pl.CostEstimate(flops=4 * 10**9, bytes_accessed=10**6, transcendentals=0)
    strip = [pltpu.VMEM((size, LANES), f32)]
    inverse, diagonal, packed = pl.pallas_call(
        first_kernel,
        out_shape=[square, stack, jax.ShapeDtypeStruct((packed_size, breadth), bf16)],
        in_specs=[pl.BlockSpec(memory_space=pltpu.HBM)] * 5,
        out_specs=[whole, anywhere, whole],
        scratch_shapes=strip
        + room
        + [
            pltpu.VMEM(points.shape, jnp.int32),
            pltpu.SMEM(rank_rows.shape, jnp.int32),
            pltpu.VMEM((1, size), jnp.int32),
            pltpu.VMEM((size, breadth), bf16),
            pltpu.VMEM((size, breadth), bf16),
            pltpu.SemaphoreType.DMA,
            pltpu.SemaphoreType.DMA((5,)),
        ],
        compiler_params=params,
        cost_estimate=estimate,
        name="first0",
    )(*(pltpu.with_memory_space_constraint(x, pltpu.HBM) for x in (points, rank_rows, labels, u_first, v_first)))
    got = packed
    pairs = hops(row_size)
    for k in range(1, blocks):
        late = lax.ppermute(got, "row", pairs[k - 1]) if k < len(pairs) else None
        inverse, diagonal = pl.pallas_call(
            functools.partial(next_kernel, k),
            out_shape=[square, stack],
            in_specs=[whole, anywhere],
            out_specs=[whole, anywhere],
            input_output_aliases={0: 0, 1: 1},
            scratch_shapes=strip + room + [pltpu.SemaphoreType.DMA],
            compiler_params=params,
            cost_estimate=estimate,
            name=f"first{k}",
        )(inverse, diagonal)
        if late is not None:
            late, inverse = lax.optimization_barrier((late, inverse))
            got = got + late

    for pair in pairs[blocks - 1 : -1]:
        got = got + lax.ppermute(got, "row", pair)
    came = lax.ppermute(got, "row", pairs[-1])

    diagonal, eliminated = pl.pallas_call(
        second_kernel,
        out_shape=[stack, jax.ShapeDtypeStruct((cycles, 1, size, NRHS), f32)],
        in_specs=[whole, scalars] + [whole] * 8 + [anywhere],
        out_specs=[anywhere, anywhere],
        scratch_shapes=[
            pltpu.VMEM((size, size), f32),
            pltpu.VMEM((blocks, size, LANES), f32),
            *room,
            pltpu.VMEM((size, NRHS), f32),
            pltpu.VMEM((size, NRHS), f32),
            pltpu.VMEM((2 * NRHS, size), bf16),
            pltpu.VMEM((2 * NRHS, size), bf16),
            pltpu.VMEM((cycles, size, NRHS), f32),
            pltpu.SemaphoreType.DMA((cycles,)),
            pltpu.SemaphoreType.DMA((blocks,)),
        ],
        input_output_aliases={10: 0},
        compiler_params=pltpu.CompilerParams(vmem_limit_bytes=40 << 20),
        name="second",
    )(
        points, rank_rows, labels, got, came, inverse,
        u_first, v_first, u_second, v_second, diagonal,
    )
    return (eliminated, diagonal)


def solution(mesh):
    in_specs = (
        P("parts", None, None),
        P("parts", "row", None),
        P("parts", "row", None),
        P("parts", "row", None, None),
        P("parts", "row", None, None),
        P("parts", "row", None, None),
        P("parts", "row", None, None),
    )
    out_specs = (P("parts", "row", None, None), P("parts", None, None))
    return jax.shard_map(
        functools.partial(local, mesh.shape["row"]),
        mesh=mesh, in_specs=in_specs, out_specs=out_specs, check_vma=False,
    )
```

```python
import functools
import math

import jax
import jax.numpy as jnp
from jax import lax
from jax.experimental import pallas as pl
from jax.experimental.pallas import tpu as pltpu
from jax.sharding import PartitionSpec as P

NRHS = 256
LANES = 128
SUB = 8
f32 = jnp.float32
bf16 = jnp.bfloat16
highest = lax.Precision.HIGHEST
high = lax.Precision.HIGH
VMEM = pltpu.VMEM
NN, TN, NT = ((1,), (0,)), ((0,), (0,)), ((1,), (1,))


def mul(left, right, dims=NN, precision=None):
    return lax.dot_general(
        left, right, (dims, ((), ())), precision=precision, preferred_element_type=f32
    )


def parts_of(value, number):
    pieces = []
    for _ in range(number):
        piece = value.astype(bf16)
        pieces.append(piece)
        value = value - piece.astype(f32)
    return pieces


def split_left(left, right, dims=NN, number=3):
    return sum(mul(piece, right, dims) for piece in reversed(parts_of(left, number)))


def split_right(left, right, dims=NN, number=3):
    return sum(mul(left, piece, dims) for piece in reversed(parts_of(right, number)))


def lower_left(product, lower, right):
    size = lower.shape[0]
    half = size // 2
    return jnp.concatenate(
        [product(lower[:half, :half], right[:half]), product(lower[half:, :], right)], axis=0
    )


def right_lower(left, lower):
    half = lower.shape[0] // 2
    return jnp.concatenate(
        [mul(left, lower[:, :half], NN, high), mul(left[:, half:], lower[half:, half:], NN, high)],
        axis=1,
    )


def right_upper(product, left, lower):
    half = lower.shape[0] // 2
    return jnp.concatenate(
        [product(left[:, :half], lower[:half, :half], NT), product(left, lower[half:, :], NT)], axis=1
    )


def row_of(value, index):
    return jnp.broadcast_to(value[index : index + 1, :], value.shape)


def column_of(value, index):
    return jnp.broadcast_to(value[:, index : index + 1], value.shape)


def tree_sum(terms):
    while len(terms) > 1:
        terms = [terms[k] + terms[k + 1] for k in range(0, len(terms), 2)]
    return terms[0]


def factor_block(rows, put):
    number = len(rows)
    lane = lax.broadcasted_iota(jnp.int32, (SUB, LANES), 1)
    sub = lax.broadcasted_iota(jnp.int32, (SUB, LANES), 0)
    pair = range(2)
    zero = jnp.zeros((SUB, LANES), f32)
    for step in range(0, number, 2):
        low = SUB * step
        here = (lane >= low) & (lane < low + 2 * SUB)
        far = step + 4
        columns = [
            [column_of(rows[i], low + c) for c in range(2 * SUB)]
            for i in range(step, min(number, far))
        ]
        pivot = [list(columns[0]), list(columns[1])]
        plain = [rows[step], rows[step + 1]]
        work = [
            jnp.where(here, jnp.where(lane - low == sub + SUB * g, 1.0, 0.0).astype(f32), plain[g])
            for g in pair
        ]
        upper, inverse, roots = [zero] * 2, [zero] * 2, [zero] * 2
        for first in range(0, 2 * SUB, 2):
            second = first + 1
            home, top, bottom = first // SUB, first % SUB, first % SUB + 1
            left, right = pivot[home][first], pivot[home][second]
            a, b, c = row_of(left, top), row_of(left, bottom), row_of(right, bottom)
            det = a * c - b * b
            scale = 1.0 / det
            is_top, is_bottom = sub == top, sub == bottom
            m_top, m_bottom = {}, {}
            for g in pair[home:]:
                p = pivot[g][first] * c - pivot[g][second] * b
                q = pivot[g][second] * a - pivot[g][first] * b
                if g == home:
                    p = jnp.where(is_top, det - c, jnp.where(is_bottom, b, p))
                    q = jnp.where(is_top, b, jnp.where(is_bottom, det - a, q))
                m_top[g], m_bottom[g] = p * scale, q * scale

            def eliminate(g, value, above, below):
                return value - m_top[g] * above - m_bottom[g] * below

            w_top, w_bottom = row_of(work[home], top), row_of(work[home], bottom)
            p_top, p_bottom = row_of(plain[home], top), row_of(plain[home], bottom)
            ratio = b * (1.0 / a)
            after = sub >= top
            upper[home] = jnp.where(
                after, jnp.where(is_top, p_top, p_bottom - ratio * p_top), upper[home]
            )
            inverse[home] = jnp.where(
                after, jnp.where(is_top, w_top, w_bottom - ratio * w_top), inverse[home]
            )
            roots[home] = jnp.where(
                after, jnp.where(is_top, lax.rsqrt(a), lax.rsqrt(c - b * ratio)), roots[home]
            )
            for other in range(second + 1, 2 * SUB):
                above, below = row_of(pivot[home][other], top), row_of(pivot[home][other], bottom)
                for g in pair[home:]:
                    pivot[g][other] = eliminate(g, pivot[g][other], above, below)
            for g in pair[home:]:
                work[g] = eliminate(g, work[g], w_top, w_bottom)
                plain[g] = eliminate(g, plain[g], p_top, p_bottom)
        for g in pair:
            put(
                step + g,
                jnp.where(lane - low >= sub + SUB * g, upper[g] * roots[g], 0.0),
                jnp.where(lane - low <= sub + SUB * g, inverse[g] * roots[g], 0.0),
            )
        if step + 2 < number:
            solved = [row_of(work[1], c) for c in range(SUB)]
            work[0] = work[0] - tree_sum([pivot[0][SUB + c] * solved[c] for c in range(SUB)])
            solved = [row_of(work[0], c) for c in range(SUB)] + solved
            if far < number:
                spread = jnp.concatenate([zero] * step + work + [zero] * (number - 2 - step), axis=0)
                change = mul(jnp.concatenate(rows[far:], axis=0), spread, NN, highest)
            for i in range(step + 2, number):
                if i < far:
                    update = tree_sum([columns[i - step][c] * solved[c] for c in range(2 * SUB)])
                else:
                    update = change[SUB * (i - far) : SUB * (i - far + 1)]
                rows[i] = jnp.where(here, 0.0, rows[i]) - update


def factor_step(matrix, strip, corner, panel, k):
    size = matrix.shape[0]
    low, top = LANES * k, LANES * (k + 1)

    def put(step, upper_rows, inverse_rows):
        at = pl.ds(SUB * step, SUB)
        corner[at, :] = upper_rows
        panel[at, low:top] = inverse_rows

    factor_block(
        [matrix[low + SUB * i : low + SUB * (i + 1), low:top] for i in range(LANES // SUB)], put
    )
    own = panel[:, low:top]
    if low:
        strip[:low, :] = jnp.zeros((low, LANES), f32)
        panel[:, :low] = mul(own, matrix[low:top, :low], NN, highest)
        matrix[low:top, :low] = panel[:, :low]
    strip[low:top, :] = corner[...].T
    matrix[low:top, low:top] = own
    if top < size:
        panel[:, top:] = mul(own, matrix[low:top, top:], NN, highest)
        matrix[low:top, top:] = jnp.zeros((LANES, size - top), f32)
        for i in range(top, size, LANES):
            strip[i : i + LANES, :] = panel[:, i : i + LANES].T
        matrix[top:, low:top] = jnp.zeros((size - top, LANES), f32)
        matrix[top:, :] = matrix[top:, :] - mul(strip[top:, :], panel[...], NN, highest)


def kernel_tile(points):
    size = points.shape[1]
    spots = points.astype(f32)
    square = jnp.sum(spots * spots, axis=0, keepdims=True)
    one = jnp.ones_like(square)
    zero = jnp.zeros((11, size), f32)
    left = jnp.concatenate([spots, square, one, zero], axis=0).astype(bf16)
    right = jnp.concatenate([-2.0 * spots, one, square, zero], axis=0).astype(bf16)
    distance = mul(left, right, TN)
    row = lax.broadcasted_iota(jnp.int32, (size, size), 0)
    column = lax.broadcasted_iota(jnp.int32, (size, size), 1)
    return lax.rsqrt(distance + 1.0) * (1.0 / (4.0 * math.pi)) + jnp.where(row == column, 1.0, 0.0)


def onehot_rows(label_row):
    size = label_row.shape[1]
    row = lax.broadcasted_iota(jnp.int32, (NRHS, size), 0).astype(f32)
    return jnp.where(row == label_row, 1.0, 0.0).astype(f32)


def pack_kernel(ranks, labels, u_first, v_first, packed, rank_rows, label_row, u_one, v_one, sems):
    size, breadth = u_one.shape
    spread = size // breadth
    position = lax.axis_index("row")
    blank = jnp.zeros((size, breadth), bf16)

    @pl.when(position > 1)
    def _():
        packed[0:size, :] = blank
        packed[size : 2 * size, :] = blank
        packed[2 * size :, :] = blank[:16]

    @pl.when(position <= 1)
    def _():
        loads = [
            pltpu.make_async_copy(source, target, sems.at[i])
            for i, (source, target) in enumerate(
                (
                    (u_first.at[0, 0], u_one),
                    (v_first.at[0, 0], v_one),
                    (labels.at[0], label_row),
                    (ranks, rank_rows),
                )
            )
        ]
        for load in loads:
            load.start()
        for load in loads:
            load.wait()
        lane = lax.broadcasted_iota(jnp.int32, (size, breadth), 1)
        own = position == 1
        packed[0:size, :] = jnp.where(own, u_one[...], 0).astype(bf16)
        packed[size : 2 * size, :] = jnp.where(own & (lane < rank_rows[0, 0]), v_one[...], 0).astype(
            bf16
        )
        label = jnp.concatenate(
            [label_row[:, breadth * i : breadth * (i + 1)].astype(f32) for i in range(spread)] * 2
            + [jnp.zeros((16 - 2 * spread, breadth), f32)],
            axis=0,
        )
        row = lax.broadcasted_iota(jnp.int32, label.shape, 0)
        source = jnp.where(row < spread, 0, 1)
        packed[2 * size :, :] = jnp.where(source == position, label, 0.0).astype(bf16)


def first_kernel(coords, matrix, diagonal, strip, corner, panel, points, sem):
    load = pltpu.make_async_copy(coords, points, sem)
    load.start()
    load.wait()
    matrix[...] = kernel_tile(points[:, 0, :])
    first_step(0, matrix, diagonal, strip, corner, panel, sem)


def next_kernel(k, old, _, matrix, diagonal, strip, corner, panel, sem):
    matrix[...] = old[...]
    first_step(k, matrix, diagonal, strip, corner, panel, sem)


def first_step(k, matrix, diagonal, strip, corner, panel, sem):
    factor_step(matrix, strip, corner, panel, k)
    copy = pltpu.make_async_copy(strip, diagonal.at[0, :, pl.ds(LANES * k, LANES)], sem)
    copy.start()
    copy.wait()


def second_kernel(
    coords, ranks, label_rows, got, came, inverse, u0, v0, u1, v1, _,
    diagonal, out,
    matrix, strip, corner, panel, y_first, y_second, z_first, z_second, result,
    out_sems, strip_sems,
):
    size = inverse.shape[0]
    cycles = result.shape[0]
    shared = (got[...].astype(f32) + came[...].astype(f32))
    u_one = shared[0:size, :].astype(bf16)
    v_one = shared[size : 2 * size, :].astype(bf16)
    labels = shared[2 * size :, :]
    spread = size // LANES

    def label_row(which):
        return jnp.concatenate(
            [labels[which * spread + i : which * spread + i + 1, :] for i in range(spread)], axis=1
        )

    first_b = onehot_rows(label_row(0)).astype(bf16)
    w_one = lower_left(split_left, inverse[...], v_one)
    w_flat = w_one.T
    gram = mul(w_flat, w_one, NN, highest)
    left = split_right(u_one, gram)
    matrix[...] = kernel_tile(coords[:, 1, :]) - split_left(left, u_one, NT)
    y0 = right_upper(split_right, first_b, inverse)
    y_first[...] = y0
    target = onehot_rows(label_row(1)) - split_left(mul(y0, w_one, NN, highest), u_one, NT)
    z0 = right_lower(y0, inverse)
    p_one = right_lower(w_flat, inverse)
    strips = []
    for k in range(size // LANES):
        factor_step(matrix, strip.at[k], corner, panel, k)
        copy = pltpu.make_async_copy(
            strip.at[k], diagonal.at[1, :, pl.ds(LANES * k, LANES)], strip_sems.at[k]
        )
        copy.start()
        strips.append(copy)
    y1 = right_upper(functools.partial(mul, precision=high), target, matrix)
    y_second[...] = y1
    z1 = right_lower(y1, matrix)
    q_one = split_left(z1, u_one, NN, 2)
    zc = z0 - mul(q_one, p_one, NN, high)
    for which, ref in ((zc, z_first), (z1, z_second)):
        big, small = parts_of(which, 2)
        ref[0:NRHS, :] = big
        ref[NRHS:, :] = small
    columns = label_rows[:, 0, :].astype(f32).T
    lane = lax.broadcasted_iota(jnp.int32, (size, LANES), 1).astype(f32)
    keep = lax.broadcasted_iota(jnp.int32, (NRHS, LANES), 1)
    position = lax.axis_index("row")
    stores = []
    for at in range(0, cycles, 2):
        tiles = range(at, min(at + 2, cycles))

        def weights(v, z, which):
            both = mul(z[...], jnp.concatenate([v[t, 0] for t in tiles], axis=1))
            value = both[:NRHS] + both[NRHS:]
            return [
                jnp.where(keep < ranks[which, t], value[:, LANES * i : LANES * (i + 1)], 0.0)
                for i, t in enumerate(tiles)
            ]

        h_first, h_second = weights(v0, z_first, 0), weights(v1, z_second, 1)
        for i, t in enumerate(tiles):
            both = jnp.concatenate([h_first[i], h_second[i]], axis=1)
            total = split_right(jnp.concatenate([u0[t, 0], u1[t, 0]], axis=1), both, NT, 2)
            column = jnp.broadcast_to(columns[:, t : t + 1], (size, LANES))
            hot = jnp.concatenate(
                [jnp.where(column == lane + float(LANES * j), 1.0, 0.0) for j in range(NRHS // LANES)],
                axis=1,
            )
            result[t] = hot - total
            if t == 0:

                @pl.when(position == 0)
                def _():
                    result[0] = y_first[...].T

                @pl.when(position == 1)
                def _():
                    result[0] = y_second[...].T

            store = pltpu.make_async_copy(result.at[t], out.at[t, 0], out_sems.at[t])
            store.start()
            stores.append(store)
    for copy in strips + stores:
        copy.wait()


def hops(number):
    chips = number // 2
    strides = [1 << b for b in range(max(chips - 1, 0).bit_length())]
    odd = strides[::-1]
    even = strides[:1] + strides[:0:-1]
    have = {0: [0], 1: [0]}
    result = []
    for index in range(len(strides)):
        pairs = []
        for core, order in ((1, odd), (0, even)):
            new = [(c, c ^ order[index]) for c in have[core] if c ^ order[index] < chips]
            pairs += [(2 * a + core, 2 * b + core) for a, b in new]
            have[core] = have[core] + [b for _, b in new]
        result.append(pairs)
    return result + [[(i, i ^ 1) for i in range(number)]]


def local(row_size, coords, labels, ranks, u_first, v_first, u_second, v_second):
    cycles, _, size, breadth = u_first.shape
    blocks = size // LANES
    whole = pl.BlockSpec(memory_space=VMEM)
    scalars = pl.BlockSpec(memory_space=pltpu.SMEM)
    anywhere = pl.BlockSpec(memory_space=pl.ANY)
    points = jnp.transpose(coords, (1, 0, 2))
    rank_rows = jnp.transpose(ranks, (1, 2, 0))[0]

    packed_size = 2 * size + 16

    square = jax.ShapeDtypeStruct((size, size), f32)
    stack = jax.ShapeDtypeStruct((2, size, size), f32)
    room = [
        pltpu.VMEM((LANES, LANES), f32),
        pltpu.VMEM((LANES, size), f32),
    ]
    params = pltpu.CompilerParams(vmem_limit_bytes=12 << 20)
    estimate = pl.CostEstimate(flops=4 * 10**9, bytes_accessed=10**6, transcendentals=0)
    strip = [pltpu.VMEM((size, LANES), f32)]
    hbm = pl.BlockSpec(memory_space=pltpu.HBM)

    def stay(*arrays):
        return tuple(pltpu.with_memory_space_constraint(x, pltpu.HBM) for x in arrays)

    got = pl.pallas_call(
        pack_kernel,
        out_shape=jax.ShapeDtypeStruct((packed_size, breadth), bf16),
        in_specs=[hbm] * 4,
        out_specs=whole,
        scratch_shapes=[
            pltpu.SMEM(rank_rows.shape, jnp.int32),
            pltpu.VMEM((1, size), jnp.int32),
            pltpu.VMEM((size, breadth), bf16),
            pltpu.VMEM((size, breadth), bf16),
            pltpu.SemaphoreType.DMA((4,)),
        ],
        compiler_params=pltpu.CompilerParams(vmem_limit_bytes=8 << 20),
        name="pack",
    )(*stay(rank_rows, labels, u_first, v_first))
    pairs = hops(row_size)
    for k in range(blocks):
        late = lax.ppermute(got, "row", pairs[k]) if k < len(pairs) - 1 else None
        inverse, diagonal = pl.pallas_call(
            functools.partial(next_kernel, k) if k else first_kernel,
            out_shape=[square, stack],
            in_specs=[whole, anywhere] if k else [hbm],
            out_specs=[whole, anywhere],
            input_output_aliases={0: 0, 1: 1} if k else {},
            scratch_shapes=strip
            + room
            + ([] if k else [pltpu.VMEM(points.shape, jnp.int32)])
            + [pltpu.SemaphoreType.DMA],
            compiler_params=params,
            cost_estimate=estimate,
            name=f"first{k}",
        )(*((inverse, diagonal) if k else stay(points)))
        if late is not None:
            late, inverse = lax.optimization_barrier((late, inverse))
            got = got + late
    for pair in pairs[blocks:-1]:
        got = got + lax.ppermute(got, "row", pair)
    came = lax.ppermute(got, "row", pairs[-1])

    diagonal, eliminated = pl.pallas_call(
        second_kernel,
        out_shape=[stack, jax.ShapeDtypeStruct((cycles, 1, size, NRHS), f32)],
        in_specs=[whole, scalars] + [whole] * 8 + [anywhere],
        out_specs=[anywhere, anywhere],
        scratch_shapes=[
            pltpu.VMEM((size, size), f32),
            pltpu.VMEM((blocks, size, LANES), f32),
            *room,
            pltpu.VMEM((NRHS, size), f32),
            pltpu.VMEM((NRHS, size), f32),
            pltpu.VMEM((2 * NRHS, size), bf16),
            pltpu.VMEM((2 * NRHS, size), bf16),
            pltpu.VMEM((cycles, size, NRHS), f32),
            pltpu.SemaphoreType.DMA((cycles,)),
            pltpu.SemaphoreType.DMA((blocks,)),
        ],
        input_output_aliases={10: 0},
        compiler_params=pltpu.CompilerParams(vmem_limit_bytes=40 << 20),
        name="second",
    )(
        points, rank_rows, labels, got, came, inverse,
        u_first, v_first, u_second, v_second, diagonal,
    )
    return (eliminated, diagonal)


def solution(mesh):
    in_specs = (
        P("parts", None, None),
        P("parts", "row", None),
        P("parts", "row", None),
        P("parts", "row", None, None),
        P("parts", "row", None, None),
        P("parts", "row", None, None),
        P("parts", "row", None, None),
    )
    out_specs = (P("parts", "row", None, None), P("parts", None, None))
    return jax.shard_map(
        functools.partial(local, mesh.shape["row"]),
        mesh=mesh, in_specs=in_specs, out_specs=out_specs, check_vma=False,
    )
```

```python
import functools
import math

import jax
import jax.numpy as jnp
from jax import lax
from jax.experimental import pallas as pl
from jax.experimental.pallas import tpu as pltpu
from jax.sharding import PartitionSpec as P

NRHS = 256
LANES = 128
SUB = 8
f32 = jnp.float32
bf16 = jnp.bfloat16
highest = lax.Precision.HIGHEST
high = lax.Precision.HIGH
VMEM = pltpu.VMEM
NN, TN, NT = ((1,), (0,)), ((0,), (0,)), ((1,), (1,))


def mul(left, right, dims=NN, precision=None):
    return lax.dot_general(
        left, right, (dims, ((), ())), precision=precision, preferred_element_type=f32
    )


def parts_of(value, number):
    pieces = []
    for _ in range(number):
        piece = value.astype(bf16)
        pieces.append(piece)
        value = value - piece.astype(f32)
    return pieces


def split_left(left, right, dims=NN, number=3):
    return sum(mul(piece, right, dims) for piece in reversed(parts_of(left, number)))


def split_right(left, right, dims=NN, number=3):
    return sum(mul(left, piece, dims) for piece in reversed(parts_of(right, number)))


def lower_left(product, lower, right):
    size = lower.shape[0]
    half = size // 2
    return jnp.concatenate(
        [product(lower[:half, :half], right[:half]), product(lower[half:, :], right)], axis=0
    )


def right_lower(left, lower):
    half = lower.shape[0] // 2
    return jnp.concatenate(
        [mul(left, lower[:, :half], NN, high), mul(left[:, half:], lower[half:, half:], NN, high)],
        axis=1,
    )


def right_upper(product, left, lower):
    half = lower.shape[0] // 2
    return jnp.concatenate(
        [product(left[:, :half], lower[:half, :half], NT), product(left, lower[half:, :], NT)], axis=1
    )


def row_of(value, index):
    return jnp.broadcast_to(value[index : index + 1, :], value.shape)


def column_of(value, index):
    return jnp.broadcast_to(value[:, index : index + 1], value.shape)


def tree_sum(terms):
    while len(terms) > 1:
        terms = [terms[k] + terms[k + 1] for k in range(0, len(terms), 2)]
    return terms[0]


def factor_block(rows, put):
    number = len(rows)
    lane = lax.broadcasted_iota(jnp.int32, (SUB, LANES), 1)
    sub = lax.broadcasted_iota(jnp.int32, (SUB, LANES), 0)
    pair = range(2)
    zero = jnp.zeros((SUB, LANES), f32)
    for step in range(0, number, 2):
        low = SUB * step
        here = (lane >= low) & (lane < low + 2 * SUB)
        far = step + 4
        columns = [
            [column_of(rows[i], low + c) for c in range(2 * SUB)]
            for i in range(step, min(number, far))
        ]
        pivot = [list(columns[0]), list(columns[1])]
        plain = [rows[step], rows[step + 1]]
        work = [
            jnp.where(here, jnp.where(lane - low == sub + SUB * g, 1.0, 0.0).astype(f32), plain[g])
            for g in pair
        ]
        upper, inverse, roots = [zero] * 2, [zero] * 2, [zero] * 2
        for first in range(0, 2 * SUB, 2):
            second = first + 1
            home, top, bottom = first // SUB, first % SUB, first % SUB + 1
            left, right = pivot[home][first], pivot[home][second]
            a, b, c = row_of(left, top), row_of(left, bottom), row_of(right, bottom)
            det = a * c - b * b
            scale = 1.0 / det
            is_top, is_bottom = sub == top, sub == bottom
            m_top, m_bottom = {}, {}
            for g in pair[home:]:
                p = pivot[g][first] * c - pivot[g][second] * b
                q = pivot[g][second] * a - pivot[g][first] * b
                if g == home:
                    p = jnp.where(is_top, det - c, jnp.where(is_bottom, b, p))
                    q = jnp.where(is_top, b, jnp.where(is_bottom, det - a, q))
                m_top[g], m_bottom[g] = p * scale, q * scale

            def eliminate(g, value, above, below):
                return value - m_top[g] * above - m_bottom[g] * below

            w_top, w_bottom = row_of(work[home], top), row_of(work[home], bottom)
            p_top, p_bottom = row_of(plain[home], top), row_of(plain[home], bottom)
            ratio = b * (1.0 / a)
            after = sub >= top
            upper[home] = jnp.where(
                after, jnp.where(is_top, p_top, p_bottom - ratio * p_top), upper[home]
            )
            inverse[home] = jnp.where(
                after, jnp.where(is_top, w_top, w_bottom - ratio * w_top), inverse[home]
            )
            roots[home] = jnp.where(
                after, jnp.where(is_top, lax.rsqrt(a), lax.rsqrt(c - b * ratio)), roots[home]
            )
            for other in range(second + 1, 2 * SUB):
                above, below = row_of(pivot[home][other], top), row_of(pivot[home][other], bottom)
                for g in pair[home:]:
                    pivot[g][other] = eliminate(g, pivot[g][other], above, below)
            for g in pair[home:]:
                work[g] = eliminate(g, work[g], w_top, w_bottom)
                plain[g] = eliminate(g, plain[g], p_top, p_bottom)
        for g in pair:
            put(
                step + g,
                jnp.where(lane - low >= sub + SUB * g, upper[g] * roots[g], 0.0),
                jnp.where(lane - low <= sub + SUB * g, inverse[g] * roots[g], 0.0),
            )
        if step + 2 < number:
            solved = [row_of(work[1], c) for c in range(SUB)]
            work[0] = work[0] - tree_sum([pivot[0][SUB + c] * solved[c] for c in range(SUB)])
            solved = [row_of(work[0], c) for c in range(SUB)] + solved
            if far < number:
                spread = jnp.concatenate([zero] * step + work + [zero] * (number - 2 - step), axis=0)
                change = mul(jnp.concatenate(rows[far:], axis=0), spread, NN, highest)
            for i in range(step + 2, number):
                if i < far:
                    update = tree_sum([columns[i - step][c] * solved[c] for c in range(2 * SUB)])
                else:
                    update = change[SUB * (i - far) : SUB * (i - far + 1)]
                rows[i] = jnp.where(here, 0.0, rows[i]) - update


def factor_step(matrix, strip, corner, panel, k, send):
    size, wide = matrix.shape
    low, top = LANES * k, LANES * (k + 1)

    def put(step, upper_rows, inverse_rows):
        at = pl.ds(SUB * step, SUB)
        corner[at, :] = upper_rows
        panel[at, low:top] = inverse_rows

    factor_block(
        [matrix[low + SUB * i : low + SUB * (i + 1), low:top] for i in range(LANES // SUB)], put
    )
    own = panel[:, low:top]
    if top < wide:
        panel[:, top:] = mul(own, matrix[low:top, top:], NN, highest)
    if low:
        strip[:low, :] = jnp.zeros((low, LANES), f32)
    strip[low:top, :] = corner[...].T
    for i in range(top, size, LANES):
        strip[i : i + LANES, :] = panel[:, i : i + LANES].T
    send()
    if low:
        panel[:, :low] = mul(own, matrix[low:top, :low], NN, highest)
    if top < size:
        matrix[top:, low:top] = jnp.zeros((size - top, LANES), f32)
        matrix[top:, :] = matrix[top:, :] - mul(strip[top:, :], panel[...], NN, highest)
        matrix[low:top, top:size] = jnp.zeros((LANES, size - top), f32)
    matrix[low:top, :top] = panel[:, :top]


def kernel_tile(points):
    size = points.shape[1]
    spots = points.astype(f32)
    square = jnp.sum(spots * spots, axis=0, keepdims=True)
    one = jnp.ones_like(square)
    zero = jnp.zeros((11, size), f32)
    left = jnp.concatenate([spots, square, one, zero], axis=0).astype(bf16)
    right = jnp.concatenate([-2.0 * spots, one, square, zero], axis=0).astype(bf16)
    distance = mul(left, right, TN)
    row = lax.broadcasted_iota(jnp.int32, (size, size), 0)
    column = lax.broadcasted_iota(jnp.int32, (size, size), 1)
    return lax.rsqrt(distance + 1.0) * (1.0 / (4.0 * math.pi)) + jnp.where(row == column, 1.0, 0.0)


def onehot_rows(label_row):
    size = label_row.shape[1]
    row = lax.broadcasted_iota(jnp.int32, (NRHS, size), 0).astype(f32)
    return jnp.where(row == label_row, 1.0, 0.0).astype(f32)


def pack_kernel(ranks, labels, u_first, v_first, packed, rank_rows, label_row, u_one, v_one, sems):
    size, breadth = u_one.shape
    spread = size // breadth
    position = lax.axis_index("row")
    blank = jnp.zeros((size, breadth), bf16)

    @pl.when(position > 1)
    def _():
        packed[0:size, :] = blank
        packed[size : 2 * size, :] = blank
        packed[2 * size :, :] = blank[:16]

    @pl.when(position <= 1)
    def _():
        loads = [
            pltpu.make_async_copy(source, target, sems.at[i])
            for i, (source, target) in enumerate(
                (
                    (u_first.at[0, 0], u_one),
                    (v_first.at[0, 0], v_one),
                    (labels.at[0], label_row),
                    (ranks, rank_rows),
                )
            )
        ]
        for load in loads:
            load.start()
        for load in loads:
            load.wait()
        lane = lax.broadcasted_iota(jnp.int32, (size, breadth), 1)
        own = position == 1
        packed[0:size, :] = jnp.where(own, u_one[...], 0).astype(bf16)
        packed[size : 2 * size, :] = jnp.where(own & (lane < rank_rows[0, 0]), v_one[...], 0).astype(
            bf16
        )
        label = jnp.concatenate(
            [label_row[:, breadth * i : breadth * (i + 1)].astype(f32) for i in range(spread)] * 2
            + [jnp.zeros((16 - 2 * spread, breadth), f32)],
            axis=0,
        )
        row = lax.broadcasted_iota(jnp.int32, label.shape, 0)
        source = jnp.where(row < spread, 0, 1)
        packed[2 * size :, :] = jnp.where(source == position, label, 0.0).astype(bf16)


def first_kernel(coords, matrix, diagonal, strip, corner, panel, points, sem):
    load = pltpu.make_async_copy(coords, points, sem)
    load.start()
    load.wait()
    matrix[...] = kernel_tile(points[:, 0, :])
    first_step(0, matrix, diagonal, strip, corner, panel, sem)


def next_kernel(k, old, _, matrix, diagonal, strip, corner, panel, sem):
    matrix[...] = old[...]
    first_step(k, matrix, diagonal, strip, corner, panel, sem)


def first_step(k, matrix, diagonal, strip, corner, panel, sem):
    copy = pltpu.make_async_copy(strip, diagonal.at[0, :, pl.ds(LANES * k, LANES)], sem)
    factor_step(matrix, strip, corner, panel, k, copy.start)
    copy.wait()


def second_kernel(
    coords, ranks, label_rows, got, came, inverse, u0, v0, u1, v1, _,
    diagonal, out,
    matrix, strip, corner, panel, y_first, y_second, z_first, z_second, result,
    out_sems, strip_sems,
):
    size = inverse.shape[0]
    cycles = result.shape[0]
    shared = (got[...].astype(f32) + came[...].astype(f32))
    u_one = shared[0:size, :].astype(bf16)
    v_one = shared[size : 2 * size, :].astype(bf16)
    labels = shared[2 * size :, :]
    spread = size // LANES

    def label_row(which):
        return jnp.concatenate(
            [labels[which * spread + i : which * spread + i + 1, :] for i in range(spread)], axis=1
        )

    w_one = lower_left(split_left, inverse[...], v_one)
    w_flat = w_one.T
    gram = mul(w_flat, w_one, NN, highest)
    left = split_right(u_one, gram)
    matrix[:, :size] = kernel_tile(coords[:, 1, :]) - split_left(left, u_one, NT)
    y0 = right_upper(split_right, onehot_rows(label_row(0)).astype(bf16), inverse)
    y_first[...] = y0
    lane = lax.broadcasted_iota(jnp.int32, (size, LANES), 1).astype(f32)

    def onehot(column):
        return jnp.concatenate(
            [jnp.where(column == lane + float(LANES * j), 1.0, 0.0) for j in range(NRHS // LANES)],
            axis=1,
        )

    own_column = jnp.broadcast_to(label_row(1), (LANES, size)).T
    weights_one = mul(y0, w_one, NN, highest).T
    matrix[:, size:] = onehot(own_column) - split_right(u_one, weights_one)
    z0 = right_lower(y0, inverse)
    p_one = right_lower(w_flat, inverse)
    strips = []
    for k in range(size // LANES):
        copy = pltpu.make_async_copy(
            strip.at[k], diagonal.at[1, :, pl.ds(LANES * k, LANES)], strip_sems.at[k]
        )
        factor_step(matrix, strip.at[k], corner, panel, k, copy.start)
        y_second[:, LANES * k : LANES * (k + 1)] = panel[:, size:].T
        strips.append(copy)
    z1 = right_lower(y_second[...], matrix.at[:, :size])
    q_one = split_left(z1, u_one, NN, 2)
    zc = z0 - mul(q_one, p_one, NN, high)
    for which, ref in ((zc, z_first), (z1, z_second)):
        big, small = parts_of(which, 2)
        ref[0:NRHS, :] = big
        ref[NRHS:, :] = small
    columns = label_rows[:, 0, :].astype(f32).T
    keep = lax.broadcasted_iota(jnp.int32, (NRHS, LANES), 1)
    position = lax.axis_index("row")
    stores = []
    for at in range(0, cycles, 2):
        tiles = range(at, min(at + 2, cycles))

        def weights(v, z, which):
            both = mul(z[...], jnp.concatenate([v[t, 0] for t in tiles], axis=1))
            value = both[:NRHS] + both[NRHS:]
            return [
                jnp.where(keep < ranks[which, t], value[:, LANES * i : LANES * (i + 1)], 0.0)
                for i, t in enumerate(tiles)
            ]

        h_first, h_second = weights(v0, z_first, 0), weights(v1, z_second, 1)
        for i, t in enumerate(tiles):
            both = jnp.concatenate([h_first[i], h_second[i]], axis=1)
            total = split_right(jnp.concatenate([u0[t, 0], u1[t, 0]], axis=1), both, NT, 2)
            column = jnp.broadcast_to(columns[:, t : t + 1], (size, LANES))
            result[t] = onehot(column) - total
            if t == 0:

                @pl.when(position == 0)
                def _():
                    result[0] = y_first[...].T

                @pl.when(position == 1)
                def _():
                    result[0] = y_second[...].T

            store = pltpu.make_async_copy(result.at[t], out.at[t, 0], out_sems.at[t])
            store.start()
            stores.append(store)
    for copy in strips + stores:
        copy.wait()


def hops(number):
    chips = number // 2
    strides = [1 << b for b in range(max(chips - 1, 0).bit_length())]
    odd = strides[::-1]
    even = strides[:1] + strides[:0:-1]
    have = {0: [0], 1: [0]}
    result = []
    for index in range(len(strides)):
        pairs = []
        for core, order in ((1, odd), (0, even)):
            new = [(c, c ^ order[index]) for c in have[core] if c ^ order[index] < chips]
            pairs += [(2 * a + core, 2 * b + core) for a, b in new]
            have[core] = have[core] + [b for _, b in new]
        result.append(pairs)
    return result + [[(i, i ^ 1) for i in range(number)]]


def local(row_size, coords, labels, ranks, u_first, v_first, u_second, v_second):
    cycles, _, size, breadth = u_first.shape
    blocks = size // LANES
    whole = pl.BlockSpec(memory_space=VMEM)
    scalars = pl.BlockSpec(memory_space=pltpu.SMEM)
    anywhere = pl.BlockSpec(memory_space=pl.ANY)
    points = jnp.transpose(coords, (1, 0, 2))
    rank_rows = jnp.transpose(ranks, (1, 2, 0))[0]

    packed_size = 2 * size + 16

    square = jax.ShapeDtypeStruct((size, size), f32)
    stack = jax.ShapeDtypeStruct((2, size, size), f32)
    room = [
        pltpu.VMEM((LANES, LANES), f32),
        pltpu.VMEM((LANES, size), f32),
    ]
    params = pltpu.CompilerParams(vmem_limit_bytes=12 << 20)
    estimate = pl.CostEstimate(flops=4 * 10**9, bytes_accessed=10**6, transcendentals=0)
    strip = [pltpu.VMEM((size, LANES), f32)]
    hbm = pl.BlockSpec(memory_space=pltpu.HBM)

    def stay(*arrays):
        return tuple(pltpu.with_memory_space_constraint(x, pltpu.HBM) for x in arrays)

    got = pl.pallas_call(
        pack_kernel,
        out_shape=jax.ShapeDtypeStruct((packed_size, breadth), bf16),
        in_specs=[hbm] * 4,
        out_specs=whole,
        scratch_shapes=[
            pltpu.SMEM(rank_rows.shape, jnp.int32),
            pltpu.VMEM((1, size), jnp.int32),
            pltpu.VMEM((size, breadth), bf16),
            pltpu.VMEM((size, breadth), bf16),
            pltpu.SemaphoreType.DMA((4,)),
        ],
        compiler_params=pltpu.CompilerParams(vmem_limit_bytes=8 << 20),
        name="pack",
    )(*stay(rank_rows, labels, u_first, v_first))
    pairs = hops(row_size)
    for k in range(blocks):
        late = lax.ppermute(got, "row", pairs[k]) if k < len(pairs) - 1 else None
        inverse, diagonal = pl.pallas_call(
            functools.partial(next_kernel, k) if k else first_kernel,
            out_shape=[square, stack],
            in_specs=[whole, anywhere] if k else [hbm],
            out_specs=[whole, anywhere],
            input_output_aliases={0: 0, 1: 1} if k else {},
            scratch_shapes=strip
            + room
            + ([] if k else [pltpu.VMEM(points.shape, jnp.int32)])
            + [pltpu.SemaphoreType.DMA],
            compiler_params=params,
            cost_estimate=estimate,
            name=f"first{k}",
        )(*((inverse, diagonal) if k else stay(points)))
        if late is not None:
            late, inverse = lax.optimization_barrier((late, inverse))
            got = got + late
    for pair in pairs[blocks:-1]:
        got = got + lax.ppermute(got, "row", pair)
    came = lax.ppermute(got, "row", pairs[-1])

    diagonal, eliminated = pl.pallas_call(
        second_kernel,
        out_shape=[stack, jax.ShapeDtypeStruct((cycles, 1, size, NRHS), f32)],
        in_specs=[whole, scalars] + [whole] * 8 + [anywhere],
        out_specs=[anywhere, anywhere],
        scratch_shapes=[
            pltpu.VMEM((size, size + NRHS), f32),
            pltpu.VMEM((blocks, size, LANES), f32),
            pltpu.VMEM((LANES, LANES), f32),
            pltpu.VMEM((LANES, size + NRHS), f32),
            pltpu.VMEM((NRHS, size), f32),
            pltpu.VMEM((NRHS, size), f32),
            pltpu.VMEM((2 * NRHS, size), bf16),
            pltpu.VMEM((2 * NRHS, size), bf16),
            pltpu.VMEM((cycles, size, NRHS), f32),
            pltpu.SemaphoreType.DMA((cycles,)),
            pltpu.SemaphoreType.DMA((blocks,)),
        ],
        input_output_aliases={10: 0},
        compiler_params=pltpu.CompilerParams(vmem_limit_bytes=40 << 20),
        name="second",
    )(
        points, rank_rows, labels, got, came, inverse,
        u_first, v_first, u_second, v_second, diagonal,
    )
    return (eliminated, diagonal)


def solution(mesh):
    in_specs = (
        P("parts", None, None),
        P("parts", "row", None),
        P("parts", "row", None),
        P("parts", "row", None, None),
        P("parts", "row", None, None),
        P("parts", "row", None, None),
        P("parts", "row", None, None),
    )
    out_specs = (P("parts", "row", None, None), P("parts", None, None))
    return jax.shard_map(
        functools.partial(local, mesh.shape["row"]),
        mesh=mesh, in_specs=in_specs, out_specs=out_specs, check_vma=False,
    )
```

```python
import functools
import math

import jax
import jax.numpy as jnp
from jax import lax
from jax.experimental import pallas as pl
from jax.experimental.pallas import tpu as pltpu
from jax.sharding import PartitionSpec as P

NRHS = 256
LANES = 128
SUB = 8
f32 = jnp.float32
bf16 = jnp.bfloat16
highest = lax.Precision.HIGHEST
high = lax.Precision.HIGH
VMEM = pltpu.VMEM
NN, TN, NT = ((1,), (0,)), ((0,), (0,)), ((1,), (1,))


def mul(left, right, dims=NN, precision=None):
    return lax.dot_general(
        left, right, (dims, ((), ())), precision=precision, preferred_element_type=f32
    )


def parts_of(value, number):
    pieces = []
    for _ in range(number):
        piece = value.astype(bf16)
        pieces.append(piece)
        value = value - piece.astype(f32)
    return pieces


def split_left(left, right, dims=NN, number=3):
    return sum(mul(piece, right, dims) for piece in reversed(parts_of(left, number)))


def split_right(left, right, dims=NN, number=3):
    return sum(mul(left, piece, dims) for piece in reversed(parts_of(right, number)))


def lower_left(product, lower, right):
    size = lower.shape[0]
    half = size // 2
    return jnp.concatenate(
        [product(lower[:half, :half], right[:half]), product(lower[half:, :], right)], axis=0
    )


def right_lower(left, lower):
    half = lower.shape[0] // 2
    return jnp.concatenate(
        [mul(left, lower[:, :half], NN, high), mul(left[:, half:], lower[half:, half:], NN, high)],
        axis=1,
    )


def right_upper(product, left, lower):
    half = lower.shape[0] // 2
    return jnp.concatenate(
        [product(left[:, :half], lower[:half, :half], NT), product(left, lower[half:, :], NT)], axis=1
    )


def row_of(value, index):
    return jnp.broadcast_to(value[index : index + 1, :], value.shape)


def column_of(value, index):
    return jnp.broadcast_to(value[:, index : index + 1], value.shape)


def tree_sum(terms):
    while len(terms) > 1:
        terms = [terms[k] + terms[k + 1] for k in range(0, len(terms), 2)]
    return terms[0]


def factor_block(rows, put):
    number = len(rows)
    lane = lax.broadcasted_iota(jnp.int32, (SUB, LANES), 1)
    sub = lax.broadcasted_iota(jnp.int32, (SUB, LANES), 0)
    pair = range(2)
    zero = jnp.zeros((SUB, LANES), f32)
    for step in range(0, number, 2):
        low = SUB * step
        here = (lane >= low) & (lane < low + 2 * SUB)
        far = step + 4
        columns = [
            [column_of(rows[i], low + c) for c in range(2 * SUB)]
            for i in range(step, min(number, far))
        ]
        pivot = [list(columns[0]), list(columns[1])]
        plain = [rows[step], rows[step + 1]]
        work = [
            jnp.where(here, jnp.where(lane - low == sub + SUB * g, 1.0, 0.0).astype(f32), plain[g])
            for g in pair
        ]
        upper, inverse, roots = [zero] * 2, [zero] * 2, [zero] * 2
        for first in range(0, 2 * SUB, 2):
            second = first + 1
            home, top, bottom = first // SUB, first % SUB, first % SUB + 1
            left, right = pivot[home][first], pivot[home][second]
            a, b, c = row_of(left, top), row_of(left, bottom), row_of(right, bottom)
            det = a * c - b * b
            scale = 1.0 / det
            is_top, is_bottom = sub == top, sub == bottom
            m_top, m_bottom = {}, {}
            for g in pair[home:]:
                p = pivot[g][first] * c - pivot[g][second] * b
                q = pivot[g][second] * a - pivot[g][first] * b
                if g == home:
                    p = jnp.where(is_top, det - c, jnp.where(is_bottom, b, p))
                    q = jnp.where(is_top, b, jnp.where(is_bottom, det - a, q))
                m_top[g], m_bottom[g] = p * scale, q * scale

            def eliminate(g, value, above, below):
                return value - m_top[g] * above - m_bottom[g] * below

            w_top, w_bottom = row_of(work[home], top), row_of(work[home], bottom)
            p_top, p_bottom = row_of(plain[home], top), row_of(plain[home], bottom)
            ratio = b * (1.0 / a)
            after = sub >= top
            upper[home] = jnp.where(
                after, jnp.where(is_top, p_top, p_bottom - ratio * p_top), upper[home]
            )
            inverse[home] = jnp.where(
                after, jnp.where(is_top, w_top, w_bottom - ratio * w_top), inverse[home]
            )
            roots[home] = jnp.where(
                after, jnp.where(is_top, lax.rsqrt(a), lax.rsqrt(c - b * ratio)), roots[home]
            )
            for other in range(second + 1, 2 * SUB):
                above, below = row_of(pivot[home][other], top), row_of(pivot[home][other], bottom)
                for g in pair[home:]:
                    pivot[g][other] = eliminate(g, pivot[g][other], above, below)
            for g in pair[home:]:
                work[g] = eliminate(g, work[g], w_top, w_bottom)
                plain[g] = eliminate(g, plain[g], p_top, p_bottom)
        for g in pair:
            put(
                step + g,
                jnp.where(lane - low >= sub + SUB * g, upper[g] * roots[g], 0.0),
                jnp.where(lane - low <= sub + SUB * g, inverse[g] * roots[g], 0.0),
            )
        if step + 2 < number:
            solved = [row_of(work[1], c) for c in range(SUB)]
            work[0] = work[0] - tree_sum([pivot[0][SUB + c] * solved[c] for c in range(SUB)])
            solved = [row_of(work[0], c) for c in range(SUB)] + solved
            if far < number:
                spread = jnp.concatenate([zero] * step + work + [zero] * (number - 2 - step), axis=0)
                change = mul(jnp.concatenate(rows[far:], axis=0), spread, NN, highest)
            for i in range(step + 2, number):
                if i < far:
                    update = tree_sum([columns[i - step][c] * solved[c] for c in range(2 * SUB)])
                else:
                    update = change[SUB * (i - far) : SUB * (i - far + 1)]
                rows[i] = jnp.where(here, 0.0, rows[i]) - update


def factor_step(matrix, strip, corner, panel, k, send):
    size, wide = matrix.shape
    low, top = LANES * k, LANES * (k + 1)

    def put(step, upper_rows, inverse_rows):
        at = pl.ds(SUB * step, SUB)
        corner[at, :] = upper_rows
        panel[at, low:top] = inverse_rows

    factor_block(
        [matrix[low + SUB * i : low + SUB * (i + 1), low:top] for i in range(LANES // SUB)], put
    )
    own = panel[:, low:top]
    if top < wide:
        panel[:, top:] = mul(own, matrix[low:top, top:], NN, high)
    if low:
        strip[:low, :] = jnp.zeros((low, LANES), f32)
    strip[low:top, :] = corner[...].T
    for i in range(top, size, LANES):
        strip[i : i + LANES, :] = panel[:, i : i + LANES].T
    send()
    if low:
        panel[:, :low] = mul(own, matrix[low:top, :low], NN, high)
    if top < size:
        matrix[top:, low:top] = jnp.zeros((size - top, LANES), f32)
        matrix[top:, :] = matrix[top:, :] - mul(strip[top:, :], panel[...], NN, high)
        matrix[low:top, top:size] = jnp.zeros((LANES, size - top), f32)
    matrix[low:top, :top] = panel[:, :top]


def kernel_tile(points):
    size = points.shape[1]
    spots = points.astype(f32)
    square = jnp.sum(spots * spots, axis=0, keepdims=True)
    one = jnp.ones_like(square)
    zero = jnp.zeros((11, size), f32)
    left = jnp.concatenate([spots, square, one, zero], axis=0).astype(bf16)
    right = jnp.concatenate([-2.0 * spots, one, square, zero], axis=0).astype(bf16)
    distance = mul(left, right, TN)
    row = lax.broadcasted_iota(jnp.int32, (size, size), 0)
    column = lax.broadcasted_iota(jnp.int32, (size, size), 1)
    return lax.rsqrt(distance + 1.0) * (1.0 / (4.0 * math.pi)) + jnp.where(row == column, 1.0, 0.0)


def onehot_rows(label_row):
    size = label_row.shape[1]
    row = lax.broadcasted_iota(jnp.int32, (NRHS, size), 0).astype(f32)
    return jnp.where(row == label_row, 1.0, 0.0).astype(f32)


def pack_kernel(ranks, labels, u_first, v_first, packed, rank_rows, label_row, u_one, v_one, sems):
    size, breadth = u_one.shape
    spread = size // breadth
    position = lax.axis_index("row")
    blank = jnp.zeros((size, breadth), bf16)

    @pl.when(position > 1)
    def _():
        packed[0:size, :] = blank
        packed[size : 2 * size, :] = blank
        packed[2 * size :, :] = blank[:16]

    @pl.when(position <= 1)
    def _():
        loads = [
            pltpu.make_async_copy(source, target, sems.at[i])
            for i, (source, target) in enumerate(
                (
                    (u_first.at[0, 0], u_one),
                    (v_first.at[0, 0], v_one),
                    (labels.at[0], label_row),
                    (ranks, rank_rows),
                )
            )
        ]
        for load in loads:
            load.start()
        for load in loads:
            load.wait()
        lane = lax.broadcasted_iota(jnp.int32, (size, breadth), 1)
        own = position == 1
        packed[0:size, :] = jnp.where(own, u_one[...], 0).astype(bf16)
        packed[size : 2 * size, :] = jnp.where(own & (lane < rank_rows[0, 0]), v_one[...], 0).astype(
            bf16
        )
        label = jnp.concatenate(
            [label_row[:, breadth * i : breadth * (i + 1)].astype(f32) for i in range(spread)] * 2
            + [jnp.zeros((16 - 2 * spread, breadth), f32)],
            axis=0,
        )
        row = lax.broadcasted_iota(jnp.int32, label.shape, 0)
        source = jnp.where(row < spread, 0, 1)
        packed[2 * size :, :] = jnp.where(source == position, label, 0.0).astype(bf16)


def first_kernel(coords, matrix, diagonal, strip, corner, panel, points, sem):
    load = pltpu.make_async_copy(coords, points, sem)
    load.start()
    load.wait()
    matrix[...] = kernel_tile(points[:, 0, :])
    first_step(0, matrix, diagonal, strip, corner, panel, sem)


def next_kernel(k, old, _, matrix, diagonal, strip, corner, panel, sem):
    matrix[...] = old[...]
    first_step(k, matrix, diagonal, strip, corner, panel, sem)


def first_step(k, matrix, diagonal, strip, corner, panel, sem):
    copy = pltpu.make_async_copy(strip, diagonal.at[0, :, pl.ds(LANES * k, LANES)], sem)
    factor_step(matrix, strip, corner, panel, k, copy.start)
    copy.wait()


def second_kernel(
    coords, ranks, label_rows, got, came, inverse, u0, v0, u1, v1, _,
    diagonal, out,
    matrix, strip, corner, panel, y_first, y_second, z_first, z_second, result,
    out_sems, strip_sems,
):
    size = inverse.shape[0]
    cycles = result.shape[0]
    shared = (got[...].astype(f32) + came[...].astype(f32))
    u_one = shared[0:size, :].astype(bf16)
    v_one = shared[size : 2 * size, :].astype(bf16)
    labels = shared[2 * size :, :]
    spread = size // LANES

    def label_row(which):
        return jnp.concatenate(
            [labels[which * spread + i : which * spread + i + 1, :] for i in range(spread)], axis=1
        )

    w_one = lower_left(split_left, inverse[...], v_one)
    w_flat = w_one.T
    gram = mul(w_flat, w_one, NN, highest)
    left = split_right(u_one, gram)
    matrix[:, :size] = kernel_tile(coords[:, 1, :]) - split_left(left, u_one, NT)
    y0 = right_upper(split_right, onehot_rows(label_row(0)).astype(bf16), inverse)
    y_first[...] = y0
    lane = lax.broadcasted_iota(jnp.int32, (size, LANES), 1).astype(f32)

    def onehot(column):
        return jnp.concatenate(
            [jnp.where(column == lane + float(LANES * j), 1.0, 0.0) for j in range(NRHS // LANES)],
            axis=1,
        )

    own_column = jnp.broadcast_to(label_row(1), (LANES, size)).T
    weights_one = mul(y0, w_one, NN, highest).T
    matrix[:, size:] = onehot(own_column) - split_right(u_one, weights_one)
    z0 = right_lower(y0, inverse)
    p_one = right_lower(w_flat, inverse)
    strips = []
    for k in range(size // LANES):
        copy = pltpu.make_async_copy(
            strip.at[k], diagonal.at[1, :, pl.ds(LANES * k, LANES)], strip_sems.at[k]
        )
        factor_step(matrix, strip.at[k], corner, panel, k, copy.start)
        y_second[:, LANES * k : LANES * (k + 1)] = panel[:, size:].T
        strips.append(copy)
    z1 = right_lower(y_second[...], matrix.at[:, :size])
    q_one = split_left(z1, u_one, NN, 2)
    zc = z0 - mul(q_one, p_one, NN, high)
    for which, ref in ((zc, z_first), (z1, z_second)):
        big, small = parts_of(which, 2)
        ref[0:NRHS, :] = big
        ref[NRHS:, :] = small
    columns = label_rows[:, 0, :].astype(f32).T
    keep = lax.broadcasted_iota(jnp.int32, (NRHS, LANES), 1)
    position = lax.axis_index("row")
    stores = []
    for at in range(0, cycles, 2):
        tiles = range(at, min(at + 2, cycles))

        def weights(v, z, which):
            both = mul(z[...], jnp.concatenate([v[t, 0] for t in tiles], axis=1))
            value = both[:NRHS] + both[NRHS:]
            return [
                jnp.where(keep < ranks[which, t], value[:, LANES * i : LANES * (i + 1)], 0.0)
                for i, t in enumerate(tiles)
            ]

        h_first, h_second = weights(v0, z_first, 0), weights(v1, z_second, 1)
        for i, t in enumerate(tiles):
            both = jnp.concatenate([h_first[i], h_second[i]], axis=1)
            total = split_right(jnp.concatenate([u0[t, 0], u1[t, 0]], axis=1), both, NT, 2)
            column = jnp.broadcast_to(columns[:, t : t + 1], (size, LANES))
            result[t] = onehot(column) - total
            if t == 0:

                @pl.when(position == 0)
                def _():
                    result[0] = y_first[...].T

                @pl.when(position == 1)
                def _():
                    result[0] = y_second[...].T

            store = pltpu.make_async_copy(result.at[t], out.at[t, 0], out_sems.at[t])
            store.start()
            stores.append(store)
    for copy in strips + stores:
        copy.wait()


def hops(number):
    chips = number // 2
    strides = [1 << b for b in range(max(chips - 1, 0).bit_length())]
    odd = strides[::-1]
    even = strides[:1] + strides[:0:-1]
    have = {0: [0], 1: [0]}
    result = []
    for index in range(len(strides)):
        pairs = []
        for core, order in ((1, odd), (0, even)):
            new = [(c, c ^ order[index]) for c in have[core] if c ^ order[index] < chips]
            pairs += [(2 * a + core, 2 * b + core) for a, b in new]
            have[core] = have[core] + [b for _, b in new]
        result.append(pairs)
    return result + [[(i, i ^ 1) for i in range(number)]]


def local(row_size, coords, labels, ranks, u_first, v_first, u_second, v_second):
    cycles, _, size, breadth = u_first.shape
    blocks = size // LANES
    whole = pl.BlockSpec(memory_space=VMEM)
    scalars = pl.BlockSpec(memory_space=pltpu.SMEM)
    anywhere = pl.BlockSpec(memory_space=pl.ANY)
    points = jnp.transpose(coords, (1, 0, 2))
    rank_rows = jnp.transpose(ranks, (1, 2, 0))[0]

    packed_size = 2 * size + 16

    square = jax.ShapeDtypeStruct((size, size), f32)
    stack = jax.ShapeDtypeStruct((2, size, size), f32)
    room = [
        pltpu.VMEM((LANES, LANES), f32),
        pltpu.VMEM((LANES, size), f32),
    ]
    params = pltpu.CompilerParams(vmem_limit_bytes=12 << 20)
    estimate = pl.CostEstimate(flops=4 * 10**9, bytes_accessed=10**6, transcendentals=0)
    strip = [pltpu.VMEM((size, LANES), f32)]
    hbm = pl.BlockSpec(memory_space=pltpu.HBM)

    def stay(*arrays):
        return tuple(pltpu.with_memory_space_constraint(x, pltpu.HBM) for x in arrays)

    got = pl.pallas_call(
        pack_kernel,
        out_shape=jax.ShapeDtypeStruct((packed_size, breadth), bf16),
        in_specs=[hbm] * 4,
        out_specs=whole,
        scratch_shapes=[
            pltpu.SMEM(rank_rows.shape, jnp.int32),
            pltpu.VMEM((1, size), jnp.int32),
            pltpu.VMEM((size, breadth), bf16),
            pltpu.VMEM((size, breadth), bf16),
            pltpu.SemaphoreType.DMA((4,)),
        ],
        compiler_params=pltpu.CompilerParams(vmem_limit_bytes=8 << 20),
        name="pack",
    )(*stay(rank_rows, labels, u_first, v_first))
    pairs = hops(row_size)
    for k in range(blocks):
        late = lax.ppermute(got, "row", pairs[k]) if k < len(pairs) - 1 else None
        inverse, diagonal = pl.pallas_call(
            functools.partial(next_kernel, k) if k else first_kernel,
            out_shape=[square, stack],
            in_specs=[whole, anywhere] if k else [hbm],
            out_specs=[whole, anywhere],
            input_output_aliases={0: 0, 1: 1} if k else {},
            scratch_shapes=strip
            + room
            + ([] if k else [pltpu.VMEM(points.shape, jnp.int32)])
            + [pltpu.SemaphoreType.DMA],
            compiler_params=params,
            cost_estimate=estimate,
            name=f"first{k}",
        )(*((inverse, diagonal) if k else stay(points)))
        if late is not None:
            late, inverse = lax.optimization_barrier((late, inverse))
            got = got + late
    for pair in pairs[blocks:-1]:
        got = got + lax.ppermute(got, "row", pair)
    came = lax.ppermute(got, "row", pairs[-1])

    diagonal, eliminated = pl.pallas_call(
        second_kernel,
        out_shape=[stack, jax.ShapeDtypeStruct((cycles, 1, size, NRHS), f32)],
        in_specs=[whole, scalars] + [whole] * 8 + [anywhere],
        out_specs=[anywhere, anywhere],
        scratch_shapes=[
            pltpu.VMEM((size, size + NRHS), f32),
            pltpu.VMEM((blocks, size, LANES), f32),
            pltpu.VMEM((LANES, LANES), f32),
            pltpu.VMEM((LANES, size + NRHS), f32),
            pltpu.VMEM((NRHS, size), f32),
            pltpu.VMEM((NRHS, size), f32),
            pltpu.VMEM((2 * NRHS, size), bf16),
            pltpu.VMEM((2 * NRHS, size), bf16),
            pltpu.VMEM((cycles, size, NRHS), f32),
            pltpu.SemaphoreType.DMA((cycles,)),
            pltpu.SemaphoreType.DMA((blocks,)),
        ],
        input_output_aliases={10: 0},
        compiler_params=pltpu.CompilerParams(vmem_limit_bytes=40 << 20),
        name="second",
    )(
        points, rank_rows, labels, got, came, inverse,
        u_first, v_first, u_second, v_second, diagonal,
    )
    return (eliminated, diagonal)


def solution(mesh):
    in_specs = (
        P("parts", None, None),
        P("parts", "row", None),
        P("parts", "row", None),
        P("parts", "row", None, None),
        P("parts", "row", None, None),
        P("parts", "row", None, None),
        P("parts", "row", None, None),
    )
    out_specs = (P("parts", "row", None, None), P("parts", None, None))
    return jax.shard_map(
        functools.partial(local, mesh.shape["row"]),
        mesh=mesh, in_specs=in_specs, out_specs=out_specs, check_vma=False,
    )
```
